512 devices in a mesh: px: 32 (over y, x), qy: 16 (over z, core).
Axes of the slice: x: 4, y: 8, z: 8, core: 2. Of those that a mesh axis runs over, the one named last changes fastest.
Arguments:
- rhs: float32 [16, 512, 8192], P(None, 'px', 'qy'), may hold values from -9 to 9
- iterate: float32 [16, 512, 8192], P(None, 'px', 'qy'), may hold values from -1.2 to 1.2
- diff_price: float32 [512, 8192], P('px', 'qy'), may hold values from 0.05 to 1
- diff_inventory: float32 [512, 8192], P('px', 'qy'), may hold values from 0.05 to 1
- drift: float32 [512, 8192], P('px', 'qy'), may hold values from 0.05 to 0.5
- boundary: int32 [512, 8192], P('px', 'qy'), may hold values 0 or 1
- drift_sign: int32 [512, 8192], P('px', 'qy'), may hold values 0 or 1
Outputs:
- solution: float32 [16, 512, 8192], P(None, 'px', 'qy')
- residual: float32 [16, 512, 8192], P(None, 'px', 'qy')
The draws below stay inside these ranges and needn't reach their ends.
All inputs are finite; a program needn't handle non-finite values. No bound on the sum of `boundary` or of `drift_sign` on one device may be relied on, other than what follows from the above.
Results may differ from the reference program's by a relative error of at most 0.0035.
Values sent between devices are 32-bit elements; how exact they have to be, the bound alone decides.
A program may use at most 64 MiB of HBM per device.

```python
import math
import jax
import jax.numpy as jnp
from jax import lax

NRHS = 16
STEPS = 4
CYCLES = 2
NX = 512
NY = 8192


def draw_rhs(key, part):
    price = jnp.arange(NX, dtype=jnp.float32) / NX
    stock = jnp.arange(NY, dtype=jnp.float32) / NY
    scale = (0.5 + price)[:, None] * (0.5 + stock)[None, :]
    base = jnp.clip(jax.random.normal(key, (NRHS, NX, NY), jnp.float32), -4.0, 4.0)
    return base * scale[None]


def place_ends(entries, key, low, high):
    dims = entries.shape
    place = [jax.random.randint(jax.random.fold_in(key, axis), (), 0, dims[axis]) for axis in range(len(dims))]
    entries = entries.at[tuple(place)].set(low)
    longest = dims.index(max(dims))
    place[longest] = (place[longest] + 1) % dims[longest]
    return entries.at[tuple(place)].set(high)


def level_of(key, extent, cuts, smallest, largest):
    factor_of = 1.0
    for axis_at, shards_of in cuts:
        heights = jax.random.uniform(jax.random.fold_in(jax.random.fold_in(key, 6), axis_at), (shards_of,), jnp.float32, smallest / len(cuts), largest / len(cuts))
        factor_of = factor_of * jnp.repeat(jnp.exp(heights), extent[axis_at] // shards_of).reshape((-1,) + (1,) * (len(extent) - 1 - axis_at))
    return factor_of


def normal_values(key, shape, deviation, bound, cuts=(), kind=jnp.bfloat16):
    drawn = jax.random.normal(key, shape, jnp.float32) * deviation
    if len(cuts) > 0:
        drawn = level_of(key, shape, cuts, -0.22, 0.18) * drawn
    return jnp.clip(drawn, min=-bound, max=bound).astype(kind)


def setup_inputs(seed: int = 0) -> dict:
    keys = jax.random.split(jax.random.key(seed), 8)
    rhs = draw_rhs(jax.random.fold_in(keys[7], 71), 0)
    iterate = normal_values(keys[1], (NRHS, NX, NY), 0.2, 1.2, ((1, 32), (2, 16)), jnp.float32)
    diff_price = jnp.clip(jnp.exp(math.log(1.0) - 2.9957323 * jax.random.uniform(keys[2], (NX, NY), jnp.float32) ** level_of(keys[2], (NX, NY), ((0, 32), (1, 16)), -0.2, 0.2)), 0.05, 1.0)
    diff_inventory = jnp.clip(jnp.exp(math.log(1.0) - 2.9957323 * jax.random.uniform(keys[3], (NX, NY), jnp.float32) ** level_of(keys[3], (NX, NY), ((0, 32), (1, 16)), -0.2, 0.2)), 0.05, 1.0)
    drift = jnp.clip(jnp.exp(math.log(0.5) - 2.3025851 * jax.random.uniform(keys[4], (NX, NY), jnp.float32) ** level_of(keys[4], (NX, NY), ((0, 32), (1, 16)), -0.2, 0.2)), 0.05, 0.5)
    boundary = place_ends((jax.random.randint(keys[5], (NX, NY), 0, 16) < 1).astype(jnp.int32), jax.random.fold_in(keys[5], 1), 0, 1)
    drift_sign = place_ends((jax.random.randint(keys[6], (NX, NY), 0, 2) < 1).astype(jnp.int32), jax.random.fold_in(keys[6], 1), 0, 1)
    return dict(rhs=rhs, iterate=iterate, diff_price=diff_price, diff_inventory=diff_inventory, drift=drift, boundary=boundary, drift_sign=drift_sign)


SIGMA = 5.5
THETA = 4.5

def coefficients(diff_price, diff_inventory, drift, boundary, drift_sign):
    active = (1 - boundary).astype(jnp.float32)
    upward = drift_sign.astype(jnp.float32)
    cdiag = 1.0 + active * (2.0 * diff_price + 2.0 * diff_inventory + drift)
    cprice = active * diff_price
    clower = active * (diff_inventory + drift * upward)
    chigher = active * (diff_inventory + drift * (1.0 - upward))
    return jnp.stack([cdiag, cprice, clower, chigher])

def operate(padded, stencil):
    center = padded[:, 1:-1, 1:-1]
    beside = padded[:, 2:, 1:-1] + padded[:, :-2, 1:-1]
    return stencil[0] * center - stencil[1] * beside - stencil[2] * padded[:, 1:-1, :-2] - stencil[3] * padded[:, 1:-1, 2:]

def apply_zero(field, stencil):
    return operate(jnp.pad(field, ((0, 0), (1, 1), (1, 1))), stencil)

def minimize(solution, residual, fields):
    count = residual.shape[0]
    flattened = [field.reshape(count, -1) for field in fields]
    krylov = jnp.concatenate(flattened[:-1], 0)
    images = THETA * jnp.concatenate(flattened[1:], 0) + SIGMA * krylov
    high = lax.Precision.HIGHEST
    gram_one = jnp.dot(images.astype(jnp.float32), images.T.astype(jnp.float32), precision=high, preferred_element_type=jnp.float32)
    lower_one = jnp.linalg.cholesky(gram_one)
    ortho = lax.linalg.triangular_solve(lower_one, images, left_side=True, lower=True)
    coeffs = jnp.dot(ortho.astype(jnp.float32), flattened[0].T.astype(jnp.float32), precision=high, preferred_element_type=jnp.float32)
    update = lax.linalg.triangular_solve(lower_one, coeffs, left_side=True, lower=True, transpose_a=True)
    new_residual = flattened[0] - jnp.dot(coeffs.T.astype(jnp.float32), ortho.astype(jnp.float32), precision=high, preferred_element_type=jnp.float32)
    new_solution = solution.reshape(count, -1) + jnp.dot(update.T.astype(jnp.float32), krylov.astype(jnp.float32), precision=high, preferred_element_type=jnp.float32)
    return (new_solution.reshape(residual.shape), new_residual.reshape(residual.shape))

def reference(rhs, iterate, diff_price, diff_inventory, drift, boundary, drift_sign):
    stencil = coefficients(diff_price, diff_inventory, drift, boundary, drift_sign)
    residual = rhs - apply_zero(iterate, stencil)
    solution = iterate
    for restart in range(CYCLES):
        fields = [residual]
        for degree in range(STEPS):
            latest = fields[-1]
            fields.append((apply_zero(latest, stencil) - SIGMA * latest) / THETA)
        solution, residual = minimize(solution, residual, fields)
    return (solution, residual)
```

```python
import jax
import jax.numpy as jnp
from jax import lax
from jax.experimental import pallas as pl
from jax.experimental.pallas import tpu as pltpu
from jax.sharding import PartitionSpec as P

STEPS = 4
CYCLES = 2
SIGMA = 5.5
THETA = 4.5
HALO = STEPS
NR = 16
ROWS = 16
COLS = 512
TILES = COLS // 128
WIDE = COLS + 128
EXT = ROWS + 2 * HALO
BASIS = NR * (STEPS + 1)
MESH = pl.DeviceIdType.MESH
F32 = jnp.float32
BF16 = jnp.bfloat16
AROUND = [(a, b) for a in (-1, 0, 1) for b in (-1, 0, 1) if (a, b) != (0, 0)]


def limbs(x):
    high = x.astype(BF16)
    rest = x - high.astype(F32)
    mid = rest.astype(BF16)
    low = (rest - mid.astype(F32)).astype(BF16)
    return high, mid, low


def pick_edges(right, left):
    lane = lax.broadcasted_iota(jnp.int32, right.shape, right.ndim - 1)
    return jnp.where(lane < 64, right, left)


def kernel(
    npx, nqy,
    rhs_hbm, x_hbm, dp_hbm, di_hbm, dr_hbm, bd_hbm, sg_hbm,
    sol_hbm, res_hbm,
    rhs_v, x_in, dp_v, di_v, dr_v, bd_v, sg_v,
    cx, cl, cr, xx, xl, xr,
    p0, hl, hr, pk, basis,
    rs_out, rs_buf, gs_buf, ag_buf, packed_v,
    in_sem, c_send, c_recv, x_send, x_recv, h_send, h_recv,
    sum_send, sum_recv,
):
    px, qy = lax.axis_index("px"), lax.axis_index("qy")

    loads = []
    pairs = [(dp_hbm, dp_v), (di_hbm, di_v), (dr_hbm, dr_v), (bd_hbm, bd_v), (sg_hbm, sg_v)]
    for src, dst in ((x_hbm, x_in), (rhs_hbm, rhs_v)):
        for c in range(TILES):
            pairs.append((src.at[:, pl.ds(c * 128, 128)], dst.at[c]))
    for n, (src, dst) in enumerate(pairs):
        load = pltpu.make_async_copy(src, dst, in_sem.at[n])
        load.start()
        loads.append(load)

    cx[...] = jnp.zeros_like(cx)
    cl[...] = jnp.zeros_like(cl)
    cr[...] = jnp.zeros_like(cr)
    for edge in (0, ROWS + 1):
        xx[edge] = jnp.zeros((NR, WIDE), F32)
    xl[...] = jnp.zeros_like(xl)
    xr[...] = jnp.zeros_like(xr)
    hl[...] = jnp.zeros_like(hl)
    hr[...] = jnp.zeros_like(hr)
    for t in range(CYCLES):
        p0[t, pl.ds(0, HALO)] = jnp.zeros((HALO, NR, WIDE), F32)
        p0[t, pl.ds(HALO + ROWS, HALO)] = jnp.zeros((HALO, NR, WIDE), F32)

    def inside(a, b):
        return (px + a >= 0) & (px + a < npx) & (qy + b >= 0) & (qy + b < nqy)

    def device(a, b):
        return {"px": px + a, "qy": qy + b}

    barrier = pltpu.get_barrier_semaphore()

    @pl.loop(1, nqy)
    def _(s):
        pl.semaphore_signal(
            barrier, inc=1, device_id={"px": px, "qy": lax.rem(qy + s, nqy)}, device_id_type=MESH
        )

    @pl.loop(1, npx)
    def _(s):
        pl.semaphore_signal(
            barrier, inc=1, device_id={"px": lax.rem(px + s, npx), "qy": qy}, device_id_type=MESH
        )

    count = nqy - 1 + npx - 1
    for a in (-1, 1):
        for b in (-1, 1):
            count += inside(a, b).astype(jnp.int32)

            @pl.when(inside(a, b))
            def _():
                pl.semaphore_signal(barrier, inc=1, device_id=device(a, b), device_id_type=MESH)

    for load in loads[: 5 + TILES]:
        load.wait()
    active = (1 - bd_v[...]).astype(F32)
    upward = sg_v[...].astype(F32)
    own = pl.ds(8, ROWS)
    cx[1, own, pl.ds(0, COLS)] = active * dp_v[...]
    cx[2, own, pl.ds(0, COLS)] = active * (di_v[...] + dr_v[...] * upward)
    cx[3, own, pl.ds(0, COLS)] = active * (di_v[...] + dr_v[...] * (1.0 - upward))

    @pl.loop(0, ROWS)
    def _(i):
        for c in range(TILES):
            xx[1 + i, :, pl.ds(c * 128, 128)] = x_in[c, pl.ds(i, NR, stride=ROWS), :]

    pl.semaphore_wait(barrier, count)

    def exchange(copies):
        for (a, b), copy in copies:
            pl.when(inside(a, b))(copy.start)

    def arrive(copies):
        for (a, b), copy in copies:
            pl.when(inside(-a, -b))(copy.wait_recv)

    def left_device(copies):
        for (a, b), copy in copies:
            pl.when(inside(a, b))(copy.wait_send)

    def remote(src, dst, send, recv, a, b):
        return pltpu.make_async_remote_copy(
            src_ref=src, dst_ref=dst, send_sem=send, recv_sem=recv,
            device_id=device(a, b), device_id_type=MESH,
        )

    field_copies, x_copies = [], []
    three = pl.ds(1, 3)
    for n, (a, b) in enumerate(AROUND):
        from_rows = {-1: pl.ds(8, 8), 0: own, 1: pl.ds(16, 8)}[a]
        to_rows = {-1: pl.ds(24, 8), 0: own, 1: pl.ds(0, 8)}[a]
        from_cols = {-1: pl.ds(0, 128), 0: pl.ds(0, COLS), 1: pl.ds(COLS - 128, 128)}[b]
        src = cx.at[three, from_rows, from_cols]
        if b == 0:
            dst = cx.at[three, to_rows, from_cols]
        else:
            dst = (cr if b < 0 else cl).at[three, to_rows]
        field_copies.append(((a, b), remote(src, dst, c_send.at[n], c_recv.at[n], a, b)))
        if a != 0 and b != 0:
            continue
        if b == 0:
            src = xx.at[1 if a < 0 else ROWS, :, from_cols]
            dst = xx.at[ROWS + 1 if a < 0 else 0, :, from_cols]
        else:
            src = xx.at[pl.ds(1, ROWS), :, from_cols]
            dst = xr if b < 0 else xl
        x_copies.append(((a, b), remote(src, dst, x_send.at[n], x_recv.at[n], a, b)))
    exchange(x_copies)
    exchange(field_copies)

    def rim_copies(t):
        copies = []
        for n, (a, b) in enumerate(AROUND):
            from_rows = {-1: pl.ds(HALO, HALO), 0: pl.ds(HALO, ROWS), 1: pl.ds(ROWS, HALO)}[a]
            to_rows = {-1: pl.ds(HALO + ROWS, HALO), 0: pl.ds(HALO, ROWS), 1: pl.ds(0, HALO)}[a]
            from_cols = {-1: pl.ds(0, 128), 0: pl.ds(0, COLS), 1: pl.ds(COLS - 128, 128)}[b]
            src = p0.at[t, from_rows, :, from_cols]
            if b == 0:
                dst = p0.at[t, to_rows, :, from_cols]
            else:
                dst = (hr if b < 0 else hl).at[t, to_rows]
            copies.append(((a, b), remote(src, dst, h_send.at[t, n], h_recv.at[t, n], a, b)))
        return copies

    def image_row(above, center, below, row):
        def field(n):
            return cx[n, pl.ds(row, 1), :]

        return (
            field(0) * center
            - field(1) * (above + below)
            - field(2) * pltpu.roll(center, 1, 1)
            - field(3) * pltpu.roll(center, WIDE - 1, 1)
        )

    for load in loads[5 + TILES :]:
        load.wait()
    arrive(x_copies)
    arrive(field_copies)
    for n in (1, 2, 3):
        cx[n, :, pl.ds(COLS, 128)] = pick_edges(cr[n], cl[n])
    cx[0] = 1.0 + 2.0 * cx[1] + cx[2] + cx[3]

    @pl.loop(0, ROWS)
    def _(i):
        xx[1 + i, :, pl.ds(COLS, 128)] = pick_edges(xr[i], xl[i])
        value = image_row(xx[i], xx[1 + i], xx[2 + i], 8 + i)
        for c in range(TILES):
            p0[0, HALO + i, :, pl.ds(c * 128, 128)] = (
                rhs_v[c, pl.ds(i, NR, stride=ROWS), :] - value[:, c * 128 : c * 128 + 128]
            )

    left_device(x_copies)
    left_device(field_copies)

    def keep_limbs(i, block, value):
        for n, limb in enumerate(limbs(value)):
            basis[i, pl.ds(n * BASIS + block * NR, NR), :] = limb

    def total(t, local):
        for j in range(nqy):
            rs_out[j] = local[2 * j : 2 * j + 2]
        rs_buf[t, qy] = rs_out[qy]

        def scatter(s):
            there = lax.rem(qy + s, nqy)
            return pltpu.make_async_remote_copy(
                src_ref=rs_out.at[there], dst_ref=rs_buf.at[t, qy],
                send_sem=sum_send.at[0], recv_sem=sum_recv.at[t, 0],
                device_id={"px": px, "qy": there}, device_id_type=MESH,
            )

        def along_px(s):
            there = lax.rem(px + s, npx)
            return pltpu.make_async_remote_copy(
                src_ref=gs_buf.at[t, px], dst_ref=gs_buf.at[t, px],
                send_sem=sum_send.at[1], recv_sem=sum_recv.at[t, 1],
                device_id={"px": there, "qy": qy}, device_id_type=MESH,
            )

        def along_qy(s):
            there = lax.rem(qy + s, nqy)
            return pltpu.make_async_remote_copy(
                src_ref=ag_buf.at[t, qy], dst_ref=ag_buf.at[t, qy],
                send_sem=sum_send.at[2], recv_sem=sum_recv.at[t, 2],
                device_id={"px": px, "qy": there}, device_id_type=MESH,
            )

        def run(copy, size, buf, phase):
            @pl.loop(1, size)
            def _(s):
                copy(s).start()

            whole = pltpu.make_async_remote_copy(
                src_ref=buf.at[t, pl.ds(0, size - 1)], dst_ref=buf.at[t, pl.ds(0, size - 1)],
                send_sem=sum_send.at[phase], recv_sem=sum_recv.at[t, phase],
                device_id={"px": px, "qy": qy}, device_id_type=MESH,
            )
            whole.wait_recv()
            whole.wait_send()

        run(scatter, nqy, rs_buf, 0)
        gs_buf[t, px] = jnp.sum(rs_buf[t], axis=0)
        run(along_px, npx, gs_buf, 1)
        ag_buf[t, qy] = jnp.sum(gs_buf[t], axis=0)
        run(along_qy, nqy, ag_buf, 2)
        for j in range(nqy):
            packed_v[pl.ds(2 * j, 2), :] = ag_buf[t, j]
        return packed_v[...]

    def solve(both):
        at = lax.broadcasted_iota(jnp.int32, both.shape, 0)
        for n in range(NR * STEPS):
            row = both[n : n + 1, :]
            row = row / both[n : n + 1, n : n + 1]
            both = jnp.where(at == n, row, both - both[:, n : n + 1] * row)
        return both

    for t in range(CYCLES):
        last = t == CYCLES - 1
        rims = rim_copies(t)
        exchange(rims)

        @pl.loop(0, ROWS)
        def _(i):
            keep_limbs(i, STEPS, p0[t, HALO + i, :, pl.ds(0, COLS)])

        arrive(rims)

        @pl.loop(0, EXT)
        def _(i):
            p0[t, i, :, pl.ds(COLS, 128)] = pick_edges(hr[t, i], hl[t, i])

        for k in range(STEPS):
            src = p0.at[t] if k == 0 else pk.at[k - 1]

            def image_at(i, src=src):
                center = src[i]
                return image_row(src[i - 1], center, src[i + 1], 8 - HALO + i), center

            if k < STEPS - 1:
                for begin, end in ((k + 1, HALO), (HALO + ROWS, EXT - k - 1)):
                    @pl.loop(begin, end)
                    def _(i):
                        image, center = image_at(i)
                        pk[k, i] = image * (1.0 / THETA) - center * (SIGMA / THETA)

            @pl.loop(HALO, HALO + ROWS)
            def _(i):
                image, center = image_at(i)
                if k < STEPS - 1:
                    pk[k, i] = image * (1.0 / THETA) - center * (SIGMA / THETA)
                keep_limbs(i - HALO, k, image[:, :COLS])

        def gram_step(i, acc):
            part = basis[i]
            return acc + lax.dot_general(
                part, part, (((1,), (1,)), ((), ())), preferred_element_type=F32
            )

        acc = lax.fori_loop(0, ROWS, gram_step, jnp.zeros((3 * BASIS, 3 * BASIS), F32))
        rows = acc[2 * BASIS :] + acc[BASIS : 2 * BASIS] + acc[:BASIS]
        gram = rows[:64, 2 * BASIS :] + rows[:64, BASIS : 2 * BASIS] + rows[:64, :BASIS]
        gram = jnp.concatenate([gram, jnp.zeros((64, 48), F32)], axis=1)
        lane = lax.broadcasted_iota(jnp.int32, (32, 128), 1)
        packed = jnp.where(lane < 80, gram[:32], pltpu.roll(gram[32:], 48, 1))
        packed = total(t, packed)
        lower = pltpu.roll(packed, 80, 1)
        square = jnp.concatenate([packed, jnp.zeros((96, 128), F32)], axis=0)
        turned = square.T
        lower = jnp.where(lane < 32, turned[32:64], lower)
        answer = solve(jnp.concatenate([packed, lower], axis=0))
        left_device(rims)

        u = [answer[NR * k : NR * (k + 1)] for k in range(STEPS)]
        e = [None] * STEPS
        e[STEPS - 1] = u[STEPS - 1]
        for k in range(STEPS - 2, -1, -1):
            e[k] = u[k] - (SIGMA / THETA) * e[k + 1]
        lane = lax.broadcasted_iota(jnp.int32, (NR, 128), 1)
        blocks = []
        for k in range(STEPS + 1):
            to_res = -u[k] if k < STEPS else jnp.zeros_like(u[0])
            if k == STEPS:
                to_sol = e[0]
            elif k < STEPS - 1:
                to_sol = e[k + 1] * (1.0 / THETA)
            else:
                to_sol = jnp.zeros_like(u[0])
            blocks.append(jnp.where(lane < 80, to_res, pltpu.roll(to_sol, NR, 1)))
        blocks.append(jnp.zeros((48, 128), F32))
        weights = jnp.concatenate(blocks, axis=0).T[64:96, :BASIS]
        high, mid, low = limbs(weights)
        two = jnp.concatenate([high, mid], axis=0)
        three_limbs = jnp.concatenate([high, mid, low], axis=0)

        @pl.loop(0, ROWS)
        def _(i):
            def product(w, n):
                return jnp.dot(
                    w, basis[i, pl.ds(n * BASIS, BASIS), :], preferred_element_type=F32
                )

            d, f, g = product(three_limbs, 0), product(two, 1), product(high, 2)
            change = ((d[64:] + f[32:] + g) + (d[32:64] + f[:32])) + d[:32]
            res = p0[t, HALO + i, :, pl.ds(0, COLS)] + change[:NR]
            sol = xx[1 + i, :, pl.ds(0, COLS)] + change[NR:]
            if last:
                for c in range(TILES):
                    rhs_v[c, pl.ds(i, NR, stride=ROWS), :] = res[:, c * 128 : c * 128 + 128]
                    x_in[c, pl.ds(i, NR, stride=ROWS), :] = sol[:, c * 128 : c * 128 + 128]
            else:
                p0[t + 1, HALO + i, :, pl.ds(0, COLS)] = res
                xx[1 + i, :, pl.ds(0, COLS)] = sol

    stores = []
    for src, dst in ((x_in, sol_hbm), (rhs_v, res_hbm)):
        for c in range(TILES):
            store = pltpu.make_async_copy(
                src.at[c], dst.at[:, pl.ds(c * 128, 128)], in_sem.at[len(stores)]
            )
            store.start()
            stores.append(store)
    for store in stores:
        store.wait()


def solution(mesh):
    npx, nqy = mesh.shape["px"], mesh.shape["qy"]

    def per_device(rhs, iterate, *fields):
        flat = jax.ShapeDtypeStruct((NR * ROWS, COLS), F32)
        vmem = pltpu.VMEM
        dma = pltpu.SemaphoreType.DMA
        sol, res = pl.pallas_call(
            lambda *refs: kernel(npx, nqy, *refs),
            out_shape=(flat, flat),
            in_specs=[pl.BlockSpec(memory_space=pl.ANY)] * 7,
            out_specs=(pl.BlockSpec(memory_space=pl.ANY),) * 2,
            scratch_shapes=[
                vmem((TILES, NR * ROWS, 128), F32),
                vmem((TILES, NR * ROWS, 128), F32),
                vmem((ROWS, COLS), F32),
                vmem((ROWS, COLS), F32),
                vmem((ROWS, COLS), F32),
                vmem((ROWS, COLS), jnp.int32),
                vmem((ROWS, COLS), jnp.int32),
                vmem((4, ROWS + 16, WIDE), F32),
                vmem((4, ROWS + 16, 128), F32),
                vmem((4, ROWS + 16, 128), F32),
                vmem((ROWS + 2, NR, WIDE), F32),
                vmem((ROWS, NR, 128), F32),
                vmem((ROWS, NR, 128), F32),
                vmem((CYCLES, EXT, NR, WIDE), F32),
                vmem((CYCLES, EXT, NR, 128), F32),
                vmem((CYCLES, EXT, NR, 128), F32),
                vmem((STEPS - 1, EXT, NR, WIDE), F32),
                vmem((ROWS, 3 * BASIS, COLS), BF16),
                vmem((nqy, 2, 128), F32),
                vmem((CYCLES, nqy, 2, 128), F32),
                vmem((CYCLES, npx, 2, 128), F32),
                vmem((CYCLES, nqy, 2, 128), F32),
                vmem((2 * nqy, 128), F32),
                dma((5 + 2 * TILES,)),
                dma((8,)), dma((8,)), dma((8,)), dma((8,)),
                dma((CYCLES, 8)), dma((CYCLES, 8)),
                dma((3,)), dma((CYCLES, 3)),
            ],
            compiler_params=pltpu.CompilerParams(
                collective_id=0, has_side_effects=True, vmem_limit_bytes=48 * 1024 * 1024
            ),
        )(rhs.reshape(NR * ROWS, COLS), iterate.reshape(NR * ROWS, COLS), *fields)
        return sol.reshape(NR, ROWS, COLS), res.reshape(NR, ROWS, COLS)

    whole, plane = P(None, "px", "qy"), P("px", "qy")
    return jax.shard_map(
        per_device, mesh=mesh, in_specs=(whole, whole) + (plane,) * 5,
        out_specs=(whole, whole), check_vma=False,
    )
```

```python
import jax
import jax.numpy as jnp
from jax import lax
from jax.experimental import pallas as pl
from jax.experimental.pallas import tpu as pltpu
from jax.sharding import PartitionSpec as P

STEPS = 4
CYCLES = 2
SIGMA = 5.5
THETA = 4.5
HALO = STEPS
NR = 16
ROWS = 16
COLS = 512
TILES = COLS // 128
WIDE = COLS + 128
EXT = ROWS + 2 * HALO
BASIS = NR * (STEPS + 1)
CORES = 2
CHIPS_X = 4
MESH = pl.DeviceIdType.MESH
F32 = jnp.float32
BF16 = jnp.bfloat16
AROUND = [(a, b) for a in (-1, 0, 1) for b in (-1, 0, 1) if (a, b) != (0, 0)]


def limbs(x):
    high = x.astype(BF16)
    rest = x - high.astype(F32)
    mid = rest.astype(BF16)
    low = (rest - mid.astype(F32)).astype(BF16)
    return high, mid, low


def lanes_of(x):
    return lax.broadcasted_iota(jnp.int32, x.shape, x.ndim - 1)


def edge_pair(first, last):
    return jnp.where(lanes_of(first) < 64, first, last)


def pack(pairs):
    packed = jnp.zeros_like(pairs[0])
    lane = lanes_of(packed)
    for n, pair in enumerate(pairs):
        packed = jnp.where(lane // 8 == n, pltpu.roll(pair, (8 * n + 4) % 128, 1), packed)
    return packed


def unpack(packed, n):
    return pltpu.roll(packed, (124 - 8 * n) % 128, 1)


def kernel(
    npx, nqy,
    rhs_hbm, x_hbm, dp_hbm, di_hbm, dr_hbm, bd_hbm, sg_hbm,
    sol_hbm, res_hbm,
    rhs_v, x_in, dp_v, di_v, dr_v, bd_v, sg_v,
    cx, ce, xx, p0, p1, p2, p3, basis,
    x_out, x_side, f_out, f_side, h_out, h_side,
    rs_out, rs_buf, as_buf, ac_buf, ag_buf, packed_v,
    in_sem, c_send, c_recv, x_send, x_recv, h_send, h_recv,
    sum_send, sum_recv,
):
    px, qy = lax.axis_index("px"), lax.axis_index("qy")
    y, x = px // CHIPS_X, px % CHIPS_X
    z, core = qy // CORES, qy % CORES
    ny, nz, nxc = npx // CHIPS_X, nqy // CORES, CHIPS_X * CORES
    xc = x * CORES + core

    def along_z(s):
        there = lax.rem(z + s, nz)
        return there, {"px": px, "qy": there * CORES + core}

    def along_y(s):
        there = lax.rem(y + s, ny)
        return there, {"px": there * CHIPS_X + x, "qy": qy}

    def along_xc(s):
        there = lax.rem(xc + s, nxc)
        return there, {"px": y * CHIPS_X + there // CORES, "qy": z * CORES + there % CORES}

    loads = []
    pairs = [(x_hbm.at[:, pl.ds(c * 128, 128)], x_in.at[c]) for c in range(TILES)]
    pairs += [(dp_hbm, dp_v), (di_hbm, di_v), (dr_hbm, dr_v), (bd_hbm, bd_v), (sg_hbm, sg_v)]
    pairs += [(rhs_hbm.at[:, pl.ds(c * 128, 128)], rhs_v.at[c]) for c in range(TILES)]
    for n, (src, dst) in enumerate(pairs):
        load = pltpu.make_async_copy(src, dst, in_sem.at[n])
        load.start()
        loads.append(load)

    for edge in (0, 24):
        cx[:, pl.ds(edge, 8), :] = jnp.zeros((3, 8, COLS), F32)
    for edge in (0, ROWS + 1):
        xx[edge] = jnp.zeros((2, 8, WIDE), F32)
    for side in (x_side, f_side, h_side):
        side[...] = jnp.zeros_like(side)
    for t in range(CYCLES):
        for edge in (0, HALO + ROWS):
            p0[t, pl.ds(edge, HALO), :, :, pl.ds(0, COLS)] = jnp.zeros((HALO, 2, 8, COLS), F32)

    def inside(a, b):
        return (px + a >= 0) & (px + a < npx) & (qy + b >= 0) & (qy + b < nqy)

    def device(a, b):
        return {"px": px + a, "qy": qy + b}

    barrier = pltpu.get_barrier_semaphore()
    count = jnp.int32(nz + ny + nxc - 3)
    for a, b in AROUND:
        count += inside(a, b).astype(jnp.int32)

        @pl.when(inside(a, b))
        def _():
            pl.semaphore_signal(barrier, inc=1, device_id=device(a, b), device_id_type=MESH)

    for along, size in ((along_z, nz), (along_y, ny), (along_xc, nxc)):
        @pl.loop(1, size)
        def _(s):
            pl.semaphore_signal(barrier, inc=1, device_id=along(s)[1], device_id_type=MESH)

    def start(copies):
        for (a, b), copy in copies:
            pl.when(inside(a, b))(copy.start)

    def arrive(copies):
        for (a, b), copy in copies:
            pl.when(inside(-a, -b))(copy.wait_recv)

    def leave(copies):
        for (a, b), copy in copies:
            pl.when(inside(a, b))(copy.wait_send)

    def remote(src, dst, send, recv, a, b):
        return (a, b), pltpu.make_async_remote_copy(
            src_ref=src, dst_ref=dst, send_sem=send, recv_sem=recv,
            device_id=device(a, b), device_id_type=MESH,
        )

    def edge_copies(out, side, send, recv, corners=True):
        beside, corner = [], []
        for n, (a, b) in enumerate(AROUND):
            if b == 0:
                continue
            s = 0 if b > 0 else 1
            if a == 0:
                beside.append(
                    remote(out, side.at[s, pl.ds(1, 2)], send.at[n], recv.at[n], a, b)
                )
            elif corners:
                from_tile, to_tile = (0, 3) if a < 0 else (1, 0)
                corner.append(
                    remote(out.at[from_tile], side.at[s, to_tile], send.at[n], recv.at[n], a, b)
                )
        return beside, corner

    def both_sides(side, tile):
        lane = lax.broadcasted_iota(jnp.int32, (8, 128), 1)
        return jnp.where(lane % 8 < 4, side[0, tile], side[1, tile])

    for load in loads[:TILES]:
        load.wait()

    def turn(i):
        for c in range(TILES):
            xx[1 + i, :, :, pl.ds(c * 128, 128)] = (
                x_in[c, pl.ds(i, NR, stride=ROWS), :].reshape(2, 8, 128)
            )

    @pl.loop(0, ROWS, unroll=4)
    def _(i):
        turn(i)

    def pack_rows(ref, first, out):
        for tile in range(2):
            pairs = []
            for i in range(8):
                for h in range(2):
                    row = first + 8 * tile + i
                    pairs.append(
                        edge_pair(ref[row, h, :, pl.ds(0, 128)], ref[row, h, :, pl.ds(COLS - 128, 128)])
                    )
            out[tile] = pack(pairs)

    pack_rows(xx, 1, x_out)
    pl.semaphore_wait(barrier, count)
    x_rows = []
    for a in (-1, 1):
        n = AROUND.index((a, 0))
        x_rows.append(remote(
            xx.at[1 if a < 0 else ROWS, :, :, pl.ds(0, COLS)],
            xx.at[ROWS + 1 if a < 0 else 0, :, :, pl.ds(0, COLS)],
            x_send.at[n], x_recv.at[n], a, 0,
        ))
    x_beside, _ = edge_copies(x_out, x_side, x_send, x_recv, corners=False)
    start(x_beside)
    start(x_rows)

    for load in loads[TILES : TILES + 5]:
        load.wait()
    active = (1 - bd_v[...]).astype(F32)
    upward = sg_v[...].astype(F32)
    price = active * dp_v[...]
    lower = active * (di_v[...] + dr_v[...] * upward)
    higher = active * (di_v[...] + dr_v[...] * (1.0 - upward))
    own = pl.ds(8, ROWS)
    for n, field in enumerate((price, lower, higher)):
        cx[n, own, :] = field
    for tile in range(2):
        rows8 = slice(8 * tile, 8 * tile + 8)
        f_out[tile] = pack([
            edge_pair(field[rows8, :128], field[rows8, COLS - 128 :])
            for field in (price, lower, higher)
        ])
    f_rows = []
    for a in (-1, 1):
        n = AROUND.index((a, 0))
        f_rows.append(remote(
            cx.at[:, pl.ds(8 if a < 0 else 16, 8), :], cx.at[:, pl.ds(24 if a < 0 else 0, 8), :],
            c_send.at[n], c_recv.at[n], a, 0,
        ))
    f_beside, f_corner = edge_copies(f_out, f_side, c_send, c_recv)
    f_copies = f_beside + f_rows + f_corner
    start(f_copies)

    def spread(n, row, value, at, width):
        ce[n, row, :, pl.ds(at, width)] = jnp.broadcast_to(value, (8, width))

    diagonal = 1.0 + 2.0 * price + lower + higher
    for n, field in enumerate((diagonal, price, lower, higher)):
        for i in range(ROWS):
            spread(n, HALO + i, field[i : i + 1], 0, COLS)

    def image_row(above, center, below, row, width):
        def field(n):
            return ce[n, row, :, pl.ds(0, width)][None]

        def cut(value):
            return value[:, :, :width]

        return (
            field(0) * cut(center)
            - field(1) * (cut(above) + cut(below))
            - field(2) * cut(pltpu.roll(center, 1, 2))
            - field(3) * cut(pltpu.roll(center, WIDE - 1, 2))
        )

    for load in loads[TILES + 5 :]:
        load.wait()
    arrive(x_beside)
    for i in range(ROWS):
        tile = both_sides(x_side, 1 + i // 8)
        for h in range(2):
            xx[1 + i, h, :, pl.ds(COLS, 128)] = unpack(tile, 2 * (i % 8) + h)
    arrive(x_rows)

    def first_residual(i):
        value = image_row(xx[i], xx[1 + i], xx[2 + i], HALO + i, COLS)
        for c in range(TILES):
            p0[0, HALO + i, :, :, pl.ds(c * 128, 128)] = (
                rhs_v[c, pl.ds(i, NR, stride=ROWS), :].reshape(2, 8, 128)
                - value[:, :, c * 128 : c * 128 + 128]
            )

    def rim_rows(t):
        copies = []
        for a in (-1, 1):
            n = AROUND.index((a, 0))
            copies.append(remote(
                p0.at[t, pl.ds(HALO if a < 0 else ROWS, HALO), :, :, pl.ds(0, COLS)],
                p0.at[t, pl.ds(HALO + ROWS if a < 0 else 0, HALO), :, :, pl.ds(0, COLS)],
                h_send.at[t, n], h_recv.at[t, n], a, 0,
            ))
        return copies

    def outer_rows_first(body, t):
        for begin in (0, ROWS - HALO):
            @pl.loop(begin, begin + HALO, unroll=4)
            def _(i):
                body(i)
        if t < CYCLES:
            start(rim_rows(t))

        @pl.loop(HALO, ROWS - HALO, unroll=4)
        def _(i):
            body(i)

    outer_rows_first(first_residual, 0)

    def total(t, local):
        for j in range(nxc):
            rs_out[j] = local[4 * j : 4 * j + 4]
        rs_buf[t, xc] = rs_out[xc]

        def phase(n, along, size, src, buf, me):
            steps = [s for d in range(size // 2, 0, -1) for s in sorted({d, size - d})]
            for s in steps:
                there, where = along(s)
                pltpu.make_async_remote_copy(
                    src_ref=src(there), dst_ref=buf.at[t, me],
                    send_sem=sum_send.at[n], recv_sem=sum_recv.at[t, n],
                    device_id=where, device_id_type=MESH,
                ).start()
            whole = pltpu.make_async_remote_copy(
                src_ref=buf.at[t, pl.ds(0, size - 1)], dst_ref=buf.at[t, pl.ds(0, size - 1)],
                send_sem=sum_send.at[n], recv_sem=sum_recv.at[t, n],
                device_id={"px": px, "qy": qy}, device_id_type=MESH,
            )
            whole.wait_recv()
            return whole

        sent = [phase(0, along_xc, nxc, lambda there: rs_out.at[there], rs_buf, xc)]
        as_buf[t, y] = jnp.sum(rs_buf[t], axis=0)
        sent.append(phase(1, along_y, ny, lambda there: as_buf.at[t, y], as_buf, y))
        ac_buf[t, z] = jnp.sum(as_buf[t], axis=0)
        sent.append(phase(2, along_z, nz, lambda there: ac_buf.at[t, z], ac_buf, z))
        ag_buf[t, xc] = jnp.sum(ac_buf[t], axis=0)
        sent.append(phase(3, along_xc, nxc, lambda there: ag_buf.at[t, xc], ag_buf, xc))
        for j in range(nxc):
            packed_v[pl.ds(4 * j, 4), :] = ag_buf[t, j]
        return packed_v[...], sent

    def solve(both):
        at = lax.broadcasted_iota(jnp.int32, both.shape, 0)
        for n in range(NR * STEPS):
            row = both[n : n + 1, :]
            row = row / both[n : n + 1, n : n + 1]
            both = jnp.where(at == n, row, both - both[:, n : n + 1] * row)
        return both

    def keep_limbs(i, block, value):
        for n, limb in enumerate(limbs(value[:, :, :COLS].reshape(NR, COLS))):
            basis[i, pl.ds(n * BASIS + block * NR, NR), :] = limb

    for t in range(CYCLES):
        last = t == CYCLES - 1
        fields = [p0.at[t], p1, p2, p3]
        rims = rim_rows(t)
        pack_rows(p0.at[t], HALO, h_out.at[t])
        beside, corner = edge_copies(h_out.at[t], h_side.at[t], h_send.at[t], h_recv.at[t])
        start(beside)
        start(corner)

        @pl.loop(0, ROWS, unroll=4)
        def _(i):
            keep_limbs(i, STEPS, p0[t, HALO + i])

        if t == 0:
            arrive(f_copies)
            for p in range(EXT):
                row = 8 - HALO + p
                tile = both_sides(f_side, row // 8)
                values = [unpack(tile, n)[row % 8 : row % 8 + 1] for n in range(3)]
                values = [1.0 + 2.0 * values[0] + values[1] + values[2]] + values
                for n, value in enumerate(values):
                    spread(n, p, value, COLS, 128)
                if HALO <= p < HALO + ROWS:
                    continue
                values = [cx[n, pl.ds(row, 1), :] for n in range(3)]
                values = [1.0 + 2.0 * values[0] + values[1] + values[2]] + values
                for n, value in enumerate(values):
                    spread(n, p, value, 0, COLS)

        def lanes_around(p):
            row = 8 - HALO + p
            tile = both_sides(h_side.at[t], row // 8)
            for h in range(2):
                p0[t, p, h, :, pl.ds(COLS, 128)] = unpack(tile, 2 * (row % 8) + h)

        def advance(k, rows, inner):
            images = [
                image_row(
                    fields[k][p - 1], fields[k][p], fields[k][p + 1], p,
                    WIDE if k < STEPS - 1 else COLS,
                )
                for p in rows
            ]
            for p, image, own_row in zip(rows, images, inner):
                if k < STEPS - 1:
                    fields[k + 1][p] = image * (1.0 / THETA) - fields[k][p] * (SIGMA / THETA)
                if own_row:
                    keep_limbs(p - HALO, k, image)

        arrive(beside)
        for p in range(HALO, HALO + ROWS):
            lanes_around(p)
        for k in range(STEPS):
            @pl.loop(0, (EXT - 10 - 2 * k) // 2)
            def _(i):
                p = HALO + 1 + k + 2 * i
                advance(k, [p, p + 1], [True, True])

        arrive(rims)
        arrive(corner)
        for begin in (0, HALO + ROWS):
            for p in range(begin, begin + HALO):
                lanes_around(p)
        for k in range(STEPS):
            for begin in (k + 1, EXT - 5 - k):
                rows = [begin + n for n in range(4)]
                inner = [HALO <= p < HALO + ROWS for p in rows]
                if k == STEPS - 1:
                    advance(k, rows, inner)
                else:
                    advance(k, rows[:2], inner[:2])
                    advance(k, rows[2:], inner[2:])

        def gram_step(i, acc):
            for n in range(4):
                part = basis[4 * i + n]
                acc = acc + lax.dot_general(
                    part, part, (((1,), (1,)), ((), ())), preferred_element_type=F32
                )
            return acc

        acc = lax.fori_loop(0, ROWS // 4, gram_step, jnp.zeros((3 * BASIS, 3 * BASIS), F32))
        rows = acc[2 * BASIS :] + acc[BASIS : 2 * BASIS] + acc[:BASIS]
        gram = rows[:64, 2 * BASIS :] + rows[:64, BASIS : 2 * BASIS] + rows[:64, :BASIS]
        gram = jnp.concatenate([gram, jnp.zeros((64, 48), F32)], axis=1)
        lane = lax.broadcasted_iota(jnp.int32, (32, 128), 1)
        packed = jnp.where(lane < 80, gram[:32], pltpu.roll(gram[32:], 48, 1))
        packed, sent = total(t, packed)
        lower = pltpu.roll(packed, 80, 1)
        square = jnp.concatenate([packed, jnp.zeros((96, 128), F32)], axis=0)
        turned = square.T
        lower = jnp.where(lane < 32, turned[32:64], lower)
        answer = solve(jnp.concatenate([packed, lower], axis=0))
        if t == 0:
            leave(x_beside + x_rows + f_copies)
        leave(rims + beside + corner)
        for whole in sent:
            whole.wait_send()

        u = [answer[NR * k : NR * (k + 1)] for k in range(STEPS)]
        e = [None] * STEPS
        e[STEPS - 1] = u[STEPS - 1]
        for k in range(STEPS - 2, -1, -1):
            e[k] = u[k] - (SIGMA / THETA) * e[k + 1]
        lane = lax.broadcasted_iota(jnp.int32, (NR, 128), 1)
        blocks = []
        for k in range(STEPS + 1):
            to_res = -u[k] if k < STEPS else jnp.zeros_like(u[0])
            if k == STEPS:
                to_sol = e[0]
            elif k < STEPS - 1:
                to_sol = e[k + 1] * (1.0 / THETA)
            else:
                to_sol = jnp.zeros_like(u[0])
            blocks.append(jnp.where(lane < 80, to_res, pltpu.roll(to_sol, NR, 1)))
        blocks.append(jnp.zeros((48, 128), F32))
        weights = jnp.concatenate(blocks, axis=0).T[64:96, :BASIS]
        high, mid, low = limbs(weights)
        two = jnp.concatenate([high, mid], axis=0)
        three = jnp.concatenate([high, mid, low], axis=0)

        def update(i):
            def product(w, n):
                return jnp.dot(
                    w, basis[i, pl.ds(n * BASIS, BASIS), :], preferred_element_type=F32
                )

            d, f, g = product(three, 0), product(two, 1), product(high, 2)
            change = ((d[64:] + f[32:] + g) + (d[32:64] + f[:32])) + d[:32]
            res = p0[t, HALO + i, :, :, pl.ds(0, COLS)] + change[:NR].reshape(2, 8, COLS)
            sol = xx[1 + i, :, :, pl.ds(0, COLS)] + change[NR:].reshape(2, 8, COLS)
            if last:
                for c in range(TILES):
                    part = slice(c * 128, c * 128 + 128)
                    rhs_v[c, pl.ds(i, NR, stride=ROWS), :] = res[:, :, part].reshape(NR, 128)
                    x_in[c, pl.ds(i, NR, stride=ROWS), :] = sol[:, :, part].reshape(NR, 128)
            else:
                p0[t + 1, HALO + i, :, :, pl.ds(0, COLS)] = res
                xx[1 + i, :, :, pl.ds(0, COLS)] = sol

        outer_rows_first(update, t + 1)

    stores = []
    for src, dst in ((x_in, sol_hbm), (rhs_v, res_hbm)):
        for c in range(TILES):
            store = pltpu.make_async_copy(
                src.at[c], dst.at[:, pl.ds(c * 128, 128)], in_sem.at[len(stores)]
            )
            store.start()
            stores.append(store)
    for store in stores:
        store.wait()


def solution(mesh):
    npx, nqy = mesh.shape["px"], mesh.shape["qy"]

    def per_device(rhs, iterate, *fields):
        flat = jax.ShapeDtypeStruct((NR * ROWS, COLS), F32)
        vmem = pltpu.VMEM
        dma = pltpu.SemaphoreType.DMA
        field = vmem((EXT, 2, 8, WIDE), F32)
        plane = vmem((ROWS, COLS), F32)
        marks = vmem((ROWS, COLS), jnp.int32)
        turned = vmem((TILES, NR * ROWS, 128), F32)
        eighth = vmem((CYCLES, 8, 4, 128), F32)
        sol, res = pl.pallas_call(
            lambda *refs: kernel(npx, nqy, *refs),
            out_shape=(flat, flat),
            in_specs=[pl.BlockSpec(memory_space=pl.ANY)] * 7,
            out_specs=(pl.BlockSpec(memory_space=pl.ANY),) * 2,
            scratch_shapes=[
                turned, turned, plane, plane, plane, marks, marks,
                vmem((3, ROWS + 16, COLS), F32),
                vmem((4, EXT, 8, WIDE), F32),
                vmem((ROWS + 2, 2, 8, WIDE), F32),
                vmem((CYCLES, EXT, 2, 8, WIDE), F32),
                field, field, field,
                vmem((ROWS, 3 * BASIS, COLS), BF16),
                vmem((2, 8, 128), F32), vmem((2, 4, 8, 128), F32),
                vmem((2, 8, 128), F32), vmem((2, 4, 8, 128), F32),
                vmem((CYCLES, 2, 8, 128), F32), vmem((CYCLES, 2, 4, 8, 128), F32),
                vmem((8, 4, 128), F32), eighth, eighth, eighth, eighth,
                vmem((32, 128), F32),
                dma((5 + 2 * TILES,)),
                dma((8,)), dma((8,)), dma((8,)), dma((8,)),
                dma((CYCLES, 8)), dma((CYCLES, 8)),
                dma((4,)), dma((CYCLES, 4)),
            ],
            compiler_params=pltpu.CompilerParams(
                collective_id=0, has_side_effects=True, vmem_limit_bytes=62 * 1024 * 1024
            ),
        )(rhs.reshape(NR * ROWS, COLS), iterate.reshape(NR * ROWS, COLS), *fields)
        return sol.reshape(NR, ROWS, COLS), res.reshape(NR, ROWS, COLS)

    whole, plane = P(None, "px", "qy"), P("px", "qy")
    return jax.shard_map(
        per_device, mesh=mesh, in_specs=(whole, whole) + (plane,) * 5,
        out_specs=(whole, whole), check_vma=False,
    )
```

```python
import jax
import jax.numpy as jnp
from jax import lax
from jax.experimental import pallas as pl
from jax.experimental.pallas import tpu as pltpu
from jax.sharding import PartitionSpec as P

STEPS = 4
CYCLES = 2
SIGMA = 5.5
THETA = 4.5
HALO = STEPS
NR = 16
ROWS = 16
COLS = 512
TILES = COLS // 128
WIDE = COLS + 128
EXT = ROWS + 2 * HALO
BASIS = NR * (STEPS + 1)
CORES = 2
CHIPS_X = 4
MESH = pl.DeviceIdType.MESH
F32 = jnp.float32
BF16 = jnp.bfloat16
AROUND = [(a, b) for a in (-1, 0, 1) for b in (-1, 0, 1) if (a, b) != (0, 0)]


def limbs(x):
    high = x.astype(BF16)
    rest = x - high.astype(F32)
    mid = rest.astype(BF16)
    low = (rest - mid.astype(F32)).astype(BF16)
    return high, mid, low


def lanes_of(x):
    return lax.broadcasted_iota(jnp.int32, x.shape, x.ndim - 1)


def edge_pair(first, last):
    return jnp.where(lanes_of(first) < 64, first, last)


def pack(pairs):
    packed = jnp.zeros_like(pairs[0])
    lane = lanes_of(packed)
    for n, pair in enumerate(pairs):
        packed = jnp.where(lane // 8 == n, pltpu.roll(pair, (8 * n + 4) % 128, 1), packed)
    return packed


def unpack(packed, n):
    return pltpu.roll(packed, (124 - 8 * n) % 128, 1)


def kernel(
    npx, nqy,
    rhs_hbm, x_hbm, dp_hbm, di_hbm, dr_hbm, bd_hbm, sg_hbm,
    sol_hbm, res_hbm,
    rhs_v, x_in, dp_v, di_v, dr_v, bd_v, sg_v,
    cx, ce, xx, p0, p1, p2, p3, basis,
    x_out, x_side, f_out, f_side, h_out, h_side,
    rs_out, rs_buf, as_buf, ac_buf, ag_buf, packed_v,
    in_sem, c_send, c_recv, x_send, x_recv, h_send, h_recv,
    sum_send, sum_recv,
):
    px, qy = lax.axis_index("px"), lax.axis_index("qy")
    y, x = px // CHIPS_X, px % CHIPS_X
    z, core = qy // CORES, qy % CORES
    ny, nz, nxc = npx // CHIPS_X, nqy // CORES, CHIPS_X * CORES
    xc = x * CORES + core

    def along_z(s):
        there = lax.rem(z + s, nz)
        return there, {"px": px, "qy": there * CORES + core}

    def along_y(s):
        there = lax.rem(y + s, ny)
        return there, {"px": there * CHIPS_X + x, "qy": qy}

    def along_xc(s):
        there = lax.rem(xc + s, nxc)
        return there, {"px": y * CHIPS_X + there // CORES, "qy": z * CORES + there % CORES}

    loads = []
    pairs = [(x_hbm.at[:, pl.ds(c * 128, 128)], x_in.at[c]) for c in range(TILES)]
    pairs += [(dp_hbm, dp_v), (di_hbm, di_v), (dr_hbm, dr_v), (bd_hbm, bd_v), (sg_hbm, sg_v)]
    pairs += [(rhs_hbm.at[:, pl.ds(c * 128, 128)], rhs_v.at[c]) for c in range(TILES)]
    for n, (src, dst) in enumerate(pairs):
        load = pltpu.make_async_copy(src, dst, in_sem.at[n])
        load.start()
        loads.append(load)

    for edge in (0, 24):
        cx[:, pl.ds(edge, 8), :] = jnp.zeros((3, 8, COLS), F32)
    for edge in (0, ROWS + 1):
        xx[edge] = jnp.zeros((2, 8, WIDE), F32)
    for side in (x_side, f_side, h_side):
        side[...] = jnp.zeros_like(side)
    for t in range(CYCLES):
        for edge in (0, HALO + ROWS):
            p0[t, pl.ds(edge, HALO), :, :, pl.ds(0, COLS)] = jnp.zeros((HALO, 2, 8, COLS), F32)

    def inside(a, b):
        return (px + a >= 0) & (px + a < npx) & (qy + b >= 0) & (qy + b < nqy)

    def device(a, b):
        return {"px": px + a, "qy": qy + b}

    barrier = pltpu.get_barrier_semaphore()
    count = jnp.int32(nz + ny + nxc - 3)
    for a, b in AROUND:
        count += inside(a, b).astype(jnp.int32)

        @pl.when(inside(a, b))
        def _():
            pl.semaphore_signal(barrier, inc=1, device_id=device(a, b), device_id_type=MESH)

    for along, size in ((along_z, nz), (along_y, ny), (along_xc, nxc)):
        @pl.loop(1, size)
        def _(s):
            pl.semaphore_signal(barrier, inc=1, device_id=along(s)[1], device_id_type=MESH)

    def start(copies):
        for (a, b), copy in copies:
            pl.when(inside(a, b))(copy.start)

    def arrive(copies):
        for (a, b), copy in copies:
            pl.when(inside(-a, -b))(copy.wait_recv)

    def leave(copies):
        for (a, b), copy in copies:
            pl.when(inside(a, b))(copy.wait_send)

    def remote(src, dst, send, recv, a, b):
        return (a, b), pltpu.make_async_remote_copy(
            src_ref=src, dst_ref=dst, send_sem=send, recv_sem=recv,
            device_id=device(a, b), device_id_type=MESH,
        )

    def edge_copies(out, side, send, recv, corners=True):
        beside, corner = [], []
        for n, (a, b) in enumerate(AROUND):
            if b == 0:
                continue
            s = 0 if b > 0 else 1
            if a == 0:
                beside.append(
                    remote(out, side.at[s, pl.ds(1, 2)], send.at[n], recv.at[n], a, b)
                )
            elif corners:
                from_tile, to_tile = (0, 3) if a < 0 else (1, 0)
                corner.append(
                    remote(out.at[from_tile], side.at[s, to_tile], send.at[n], recv.at[n], a, b)
                )
        return beside, corner

    def both_sides(side, tile):
        lane = lax.broadcasted_iota(jnp.int32, (8, 128), 1)
        return jnp.where(lane % 8 < 4, side[0, tile], side[1, tile])

    for load in loads[:TILES]:
        load.wait()

    def turn(i):
        for c in range(TILES):
            xx[1 + i, :, :, pl.ds(c * 128, 128)] = (
                x_in[c, pl.ds(i, NR, stride=ROWS), :].reshape(2, 8, 128)
            )

    @pl.loop(0, ROWS, unroll=4)
    def _(i):
        turn(i)

    def pack_rows(ref, first, out):
        for tile in range(2):
            pairs = []
            for i in range(8):
                for h in range(2):
                    row = first + 8 * tile + i
                    pairs.append(
                        edge_pair(ref[row, h, :, pl.ds(0, 128)], ref[row, h, :, pl.ds(COLS - 128, 128)])
                    )
            out[tile] = pack(pairs)

    pack_rows(xx, 1, x_out)
    pl.semaphore_wait(barrier, count)
    x_rows = []
    for a in (-1, 1):
        n = AROUND.index((a, 0))
        x_rows.append(remote(
            xx.at[1 if a < 0 else ROWS, :, :, pl.ds(0, COLS)],
            xx.at[ROWS + 1 if a < 0 else 0, :, :, pl.ds(0, COLS)],
            x_send.at[n], x_recv.at[n], a, 0,
        ))
    x_beside, _ = edge_copies(x_out, x_side, x_send, x_recv, corners=False)
    start(x_beside)
    start(x_rows)

    for load in loads[TILES : TILES + 5]:
        load.wait()
    active = (1 - bd_v[...]).astype(F32)
    upward = sg_v[...].astype(F32)
    price = active * dp_v[...]
    lower = active * (di_v[...] + dr_v[...] * upward)
    higher = active * (di_v[...] + dr_v[...] * (1.0 - upward))
    own = pl.ds(8, ROWS)
    for n, field in enumerate((price, lower, higher)):
        cx[n, own, :] = field
    for tile in range(2):
        rows8 = slice(8 * tile, 8 * tile + 8)
        f_out[tile] = pack([
            edge_pair(field[rows8, :128], field[rows8, COLS - 128 :])
            for field in (price, lower, higher)
        ])
    f_rows = []
    for a in (-1, 1):
        n = AROUND.index((a, 0))
        f_rows.append(remote(
            cx.at[:, pl.ds(8 if a < 0 else 16, 8), :], cx.at[:, pl.ds(24 if a < 0 else 0, 8), :],
            c_send.at[n], c_recv.at[n], a, 0,
        ))
    f_beside, f_corner = edge_copies(f_out, f_side, c_send, c_recv)
    f_copies = f_beside + f_rows + f_corner
    start(f_copies)

    def spread(n, row, value, at, width):
        ce[n, row, :, pl.ds(at, width)] = jnp.broadcast_to(value, (8, width))

    diagonal = 1.0 + 2.0 * price + lower + higher
    for n, field in enumerate((diagonal, price, lower, higher)):
        for i in range(ROWS):
            spread(n, HALO + i, field[i : i + 1], 0, COLS)

    def image_row(above, center, below, row, width):
        def field(n):
            return ce[n, row, :, pl.ds(0, width)][None]

        def cut(value):
            return value[:, :, :width]

        return (
            field(0) * cut(center)
            - field(1) * (cut(above) + cut(below))
            - field(2) * cut(pltpu.roll(center, 1, 2))
            - field(3) * cut(pltpu.roll(center, WIDE - 1, 2))
        )

    for load in loads[TILES + 5 :]:
        load.wait()
    arrive(x_beside)
    for i in range(ROWS):
        tile = both_sides(x_side, 1 + i // 8)
        for h in range(2):
            xx[1 + i, h, :, pl.ds(COLS, 128)] = unpack(tile, 2 * (i % 8) + h)
    arrive(x_rows)

    def first_residual(i):
        value = image_row(xx[i], xx[1 + i], xx[2 + i], HALO + i, COLS)
        for c in range(TILES):
            p0[0, HALO + i, :, :, pl.ds(c * 128, 128)] = (
                rhs_v[c, pl.ds(i, NR, stride=ROWS), :].reshape(2, 8, 128)
                - value[:, :, c * 128 : c * 128 + 128]
            )

    def rim_rows(t):
        copies = []
        for a in (-1, 1):
            n = AROUND.index((a, 0))
            copies.append(remote(
                p0.at[t, pl.ds(HALO if a < 0 else ROWS, HALO), :, :, pl.ds(0, COLS)],
                p0.at[t, pl.ds(HALO + ROWS if a < 0 else 0, HALO), :, :, pl.ds(0, COLS)],
                h_send.at[t, n], h_recv.at[t, n], a, 0,
            ))
        return copies

    def outer_rows_first(body, t):
        for begin in (0, ROWS - HALO):
            @pl.loop(begin, begin + HALO, unroll=4)
            def _(i):
                body(i)
        if t < CYCLES:
            start(rim_rows(t))

        @pl.loop(HALO, ROWS - HALO, unroll=4)
        def _(i):
            body(i)

    outer_rows_first(first_residual, 0)

    def total(t, local):
        for j in range(nxc):
            rs_out[j] = local[4 * j : 4 * j + 4]
        rs_buf[t, xc] = rs_out[xc]

        def phase(n, along, size, src, buf, me):
            steps = [s for d in range(size // 2, 0, -1) for s in sorted({d, size - d})]
            for s in steps:
                there, where = along(s)
                pltpu.make_async_remote_copy(
                    src_ref=src(there), dst_ref=buf.at[t, me],
                    send_sem=sum_send.at[n], recv_sem=sum_recv.at[t, n],
                    device_id=where, device_id_type=MESH,
                ).start()
            whole = pltpu.make_async_remote_copy(
                src_ref=buf.at[t, pl.ds(0, size - 1)], dst_ref=buf.at[t, pl.ds(0, size - 1)],
                send_sem=sum_send.at[n], recv_sem=sum_recv.at[t, n],
                device_id={"px": px, "qy": qy}, device_id_type=MESH,
            )
            whole.wait_recv()
            return whole

        sent = [phase(0, along_xc, nxc, lambda there: rs_out.at[there], rs_buf, xc)]
        as_buf[t, y] = jnp.sum(rs_buf[t], axis=0)
        sent.append(phase(1, along_y, ny, lambda there: as_buf.at[t, y], as_buf, y))
        ac_buf[t, z] = jnp.sum(as_buf[t], axis=0)
        sent.append(phase(2, along_z, nz, lambda there: ac_buf.at[t, z], ac_buf, z))
        ag_buf[t, xc] = jnp.sum(ac_buf[t], axis=0)
        sent.append(phase(3, along_xc, nxc, lambda there: ag_buf.at[t, xc], ag_buf, xc))
        for j in range(nxc):
            packed_v[pl.ds(4 * j, 4), :] = ag_buf[t, j]
        return packed_v[...], sent

    def solve(both):
        tiles = [both[8 * r : 8 * r + 8] for r in range(8)]
        at = lax.broadcasted_iota(jnp.int32, (8, 128), 0)

        def across(row):
            return jnp.broadcast_to(row, (8, 128))

        for b in range(8):
            columns = [
                [jnp.broadcast_to(tile[:, n : n + 1], (8, 128)) for tile in tiles]
                for n in range(8 * b, 8 * b + 8)
            ]
            for j in range(8):
                pivots = columns[j]
                inverse = 1.0 / across(pivots[b][j : j + 1])

                def eliminate(group):
                    row = across(group[b][j : j + 1]) * inverse
                    after = [g - c * row for g, c in zip(group, pivots)]
                    after[b] = jnp.where(at == j, row, after[b])
                    return after

                for q in range(j + 1, 8):
                    columns[q] = eliminate(columns[q])
                tiles = eliminate(tiles)
        return jnp.concatenate(tiles, axis=0)

    def keep_limbs(i, block, value):
        for n, limb in enumerate(limbs(value[:, :, :COLS].reshape(NR, COLS))):
            basis[i, pl.ds(n * BASIS + block * NR, NR), :] = limb

    for t in range(CYCLES):
        last = t == CYCLES - 1
        fields = [p0.at[t], p1, p2, p3]
        rims = rim_rows(t)
        pack_rows(p0.at[t], HALO, h_out.at[t])
        beside, corner = edge_copies(h_out.at[t], h_side.at[t], h_send.at[t], h_recv.at[t])
        start(beside)
        start(corner)

        @pl.loop(0, ROWS, unroll=4)
        def _(i):
            keep_limbs(i, STEPS, p0[t, HALO + i])

        if t == 0:
            arrive(f_copies)
            for p in range(EXT):
                row = 8 - HALO + p
                tile = both_sides(f_side, row // 8)
                values = [unpack(tile, n)[row % 8 : row % 8 + 1] for n in range(3)]
                values = [1.0 + 2.0 * values[0] + values[1] + values[2]] + values
                for n, value in enumerate(values):
                    spread(n, p, value, COLS, 128)
                if HALO <= p < HALO + ROWS:
                    continue
                values = [cx[n, pl.ds(row, 1), :] for n in range(3)]
                values = [1.0 + 2.0 * values[0] + values[1] + values[2]] + values
                for n, value in enumerate(values):
                    spread(n, p, value, 0, COLS)

        def lanes_around(p):
            row = 8 - HALO + p
            tile = both_sides(h_side.at[t], row // 8)
            for h in range(2):
                p0[t, p, h, :, pl.ds(COLS, 128)] = unpack(tile, 2 * (row % 8) + h)

        def advance(k, rows, inner):
            images = [
                image_row(
                    fields[k][p - 1], fields[k][p], fields[k][p + 1], p,
                    WIDE if k < STEPS - 1 else COLS,
                )
                for p in rows
            ]
            for p, image, own_row in zip(rows, images, inner):
                if k < STEPS - 1:
                    fields[k + 1][p] = image * (1.0 / THETA) - fields[k][p] * (SIGMA / THETA)
                if own_row:
                    keep_limbs(p - HALO, k, image)

        arrive(beside)
        for p in range(HALO, HALO + ROWS):
            lanes_around(p)
        for k in range(STEPS):
            @pl.loop(0, (EXT - 10 - 2 * k) // 2)
            def _(i):
                p = HALO + 1 + k + 2 * i
                advance(k, [p, p + 1], [True, True])

        def gram_step(i, acc):
            for n in range(4):
                part = basis[4 * i + n]
                acc = acc + lax.dot_general(
                    part, part, (((1,), (1,)), ((), ())), preferred_element_type=F32
                )
            return acc

        acc = lax.fori_loop(1, 3, gram_step, jnp.zeros((3 * BASIS, 3 * BASIS), F32))

        arrive(rims)
        arrive(corner)
        for begin in (0, HALO + ROWS):
            for p in range(begin, begin + HALO):
                lanes_around(p)
        for k in range(STEPS):
            for begin in (k + 1, EXT - 5 - k):
                rows = [begin + n for n in range(4)]
                inner = [HALO <= p < HALO + ROWS for p in rows]
                if k == STEPS - 1:
                    advance(k, rows, inner)
                else:
                    advance(k, rows[:2], inner[:2])
                    advance(k, rows[2:], inner[2:])

        acc = gram_step(3, gram_step(0, acc))
        rows = acc[2 * BASIS :] + acc[BASIS : 2 * BASIS] + acc[:BASIS]
        gram = rows[:64, 2 * BASIS :] + rows[:64, BASIS : 2 * BASIS] + rows[:64, :BASIS]
        gram = jnp.concatenate([gram, jnp.zeros((64, 48), F32)], axis=1)
        lane = lax.broadcasted_iota(jnp.int32, (32, 128), 1)
        packed = jnp.where(lane < 80, gram[:32], pltpu.roll(gram[32:], 48, 1))
        packed, sent = total(t, packed)
        lower = pltpu.roll(packed, 80, 1)
        square = jnp.concatenate([packed, jnp.zeros((96, 128), F32)], axis=0)
        turned = square.T
        lower = jnp.where(lane < 32, turned[32:64], lower)
        answer = solve(jnp.concatenate([packed, lower], axis=0))
        if t == 0:
            leave(x_beside + x_rows + f_copies)
        leave(rims + beside + corner)
        for whole in sent:
            whole.wait_send()

        u = [answer[NR * k : NR * (k + 1)] for k in range(STEPS)]
        e = [None] * STEPS
        e[STEPS - 1] = u[STEPS - 1]
        for k in range(STEPS - 2, -1, -1):
            e[k] = u[k] - (SIGMA / THETA) * e[k + 1]
        lane = lax.broadcasted_iota(jnp.int32, (NR, 128), 1)
        blocks = []
        for k in range(STEPS + 1):
            to_res = -u[k] if k < STEPS else jnp.zeros_like(u[0])
            if k == STEPS:
                to_sol = e[0]
            elif k < STEPS - 1:
                to_sol = e[k + 1] * (1.0 / THETA)
            else:
                to_sol = jnp.zeros_like(u[0])
            blocks.append(jnp.where(lane < 80, to_res, pltpu.roll(to_sol, NR, 1)))
        blocks.append(jnp.zeros((48, 128), F32))
        weights = jnp.concatenate(blocks, axis=0).T[64:96, :BASIS]
        high, mid, low = limbs(weights)
        two = jnp.concatenate([high, mid], axis=0)
        three = jnp.concatenate([high, mid, low], axis=0)

        def update(i):
            def product(w, n):
                return jnp.dot(
                    w, basis[i, pl.ds(n * BASIS, BASIS), :], preferred_element_type=F32
                )

            d, f, g = product(three, 0), product(two, 1), product(high, 2)
            change = ((d[64:] + f[32:] + g) + (d[32:64] + f[:32])) + d[:32]
            res = p0[t, HALO + i, :, :, pl.ds(0, COLS)] + change[:NR].reshape(2, 8, COLS)
            sol = xx[1 + i, :, :, pl.ds(0, COLS)] + change[NR:].reshape(2, 8, COLS)
            if last:
                for c in range(TILES):
                    part = slice(c * 128, c * 128 + 128)
                    rhs_v[c, pl.ds(i, NR, stride=ROWS), :] = res[:, :, part].reshape(NR, 128)
                    x_in[c, pl.ds(i, NR, stride=ROWS), :] = sol[:, :, part].reshape(NR, 128)
            else:
                p0[t + 1, HALO + i, :, :, pl.ds(0, COLS)] = res
                xx[1 + i, :, :, pl.ds(0, COLS)] = sol

        outer_rows_first(update, t + 1)

    stores = []
    for src, dst in ((x_in, sol_hbm), (rhs_v, res_hbm)):
        for c in range(TILES):
            store = pltpu.make_async_copy(
                src.at[c], dst.at[:, pl.ds(c * 128, 128)], in_sem.at[len(stores)]
            )
            store.start()
            stores.append(store)
    for store in stores:
        store.wait()


def solution(mesh):
    npx, nqy = mesh.shape["px"], mesh.shape["qy"]

    def per_device(rhs, iterate, *fields):
        flat = jax.ShapeDtypeStruct((NR * ROWS, COLS), F32)
        vmem = pltpu.VMEM
        dma = pltpu.SemaphoreType.DMA
        field = vmem((EXT, 2, 8, WIDE), F32)
        plane = vmem((ROWS, COLS), F32)
        marks = vmem((ROWS, COLS), jnp.int32)
        turned = vmem((TILES, NR * ROWS, 128), F32)
        eighth = vmem((CYCLES, 8, 4, 128), F32)
        sol, res = pl.pallas_call(
            lambda *refs: kernel(npx, nqy, *refs),
            out_shape=(flat, flat),
            in_specs=[pl.BlockSpec(memory_space=pl.ANY)] * 7,
            out_specs=(pl.BlockSpec(memory_space=pl.ANY),) * 2,
            scratch_shapes=[
                turned, turned, plane, plane, plane, marks, marks,
                vmem((3, ROWS + 16, COLS), F32),
                vmem((4, EXT, 8, WIDE), F32),
                vmem((ROWS + 2, 2, 8, WIDE), F32),
                vmem((CYCLES, EXT, 2, 8, WIDE), F32),
                field, field, field,
                vmem((ROWS, 3 * BASIS, COLS), BF16),
                vmem((2, 8, 128), F32), vmem((2, 4, 8, 128), F32),
                vmem((2, 8, 128), F32), vmem((2, 4, 8, 128), F32),
                vmem((CYCLES, 2, 8, 128), F32), vmem((CYCLES, 2, 4, 8, 128), F32),
                vmem((8, 4, 128), F32), eighth, eighth, eighth, eighth,
                vmem((32, 128), F32),
                dma((5 + 2 * TILES,)),
                dma((8,)), dma((8,)), dma((8,)), dma((8,)),
                dma((CYCLES, 8)), dma((CYCLES, 8)),
                dma((4,)), dma((CYCLES, 4)),
            ],
            compiler_params=pltpu.CompilerParams(
                collective_id=0, has_side_effects=True, vmem_limit_bytes=62 * 1024 * 1024
            ),
        )(rhs.reshape(NR * ROWS, COLS), iterate.reshape(NR * ROWS, COLS), *fields)
        return sol.reshape(NR, ROWS, COLS), res.reshape(NR, ROWS, COLS)

    whole, plane = P(None, "px", "qy"), P("px", "qy")
    return jax.shard_map(
        per_device, mesh=mesh, in_specs=(whole, whole) + (plane,) * 5,
        out_specs=(whole, whole), check_vma=False,
    )
```

```python
import jax
import jax.numpy as jnp
from jax import lax
from jax.experimental import pallas as pl
from jax.experimental.pallas import tpu as pltpu
from jax.sharding import PartitionSpec as P

STEPS = 4
CYCLES = 2
SIGMA = 5.5
THETA = 4.5
HALO = STEPS
NR = 16
ROWS = 16
COLS = 512
TILES = COLS // 128
WIDE = COLS + 128
EXT = ROWS + 2 * HALO
BASIS = NR * (STEPS + 1)
CORES = 2
CHIPS_X = 4
MESH = pl.DeviceIdType.MESH
F32 = jnp.float32
BF16 = jnp.bfloat16
AROUND = [(a, b) for a in (-1, 0, 1) for b in (-1, 0, 1) if (a, b) != (0, 0)]


def limbs(x):
    high = x.astype(BF16)
    rest = x - high.astype(F32)
    mid = rest.astype(BF16)
    low = (rest - mid.astype(F32)).astype(BF16)
    return high, mid, low


def lanes_of(x):
    return lax.broadcasted_iota(jnp.int32, x.shape, x.ndim - 1)


def edge_pair(first, last):
    return jnp.where(lanes_of(first) < 64, first, last)


def pack(pairs):
    packed = jnp.zeros_like(pairs[0])
    lane = lanes_of(packed)
    for n, pair in enumerate(pairs):
        packed = jnp.where(lane // 8 == n, pltpu.roll(pair, (8 * n + 4) % 128, 1), packed)
    return packed


def unpack(packed, n):
    return pltpu.roll(packed, (124 - 8 * n) % 128, 1)


def kernel(
    npx, nqy,
    rhs_hbm, x_hbm, dp_hbm, di_hbm, dr_hbm, bd_hbm, sg_hbm,
    sol_hbm, res_hbm,
    rhs_v, x_in, dp_v, di_v, dr_v, bd_v, sg_v,
    cx, ce, xx, p0, p1, p2, p3, basis,
    x_out, x_side, f_out, f_side, h_out, h_side,
    rs_out, rs_buf, as_buf, ag_buf, packed_v,
    in_sem, c_send, c_recv, x_send, x_recv, h_send, h_recv,
    sum_send, sum_recv,
):
    px, qy = lax.axis_index("px"), lax.axis_index("qy")
    y, x = px // CHIPS_X, px % CHIPS_X
    z, core = qy // CORES, qy % CORES
    ny, nz = npx // CHIPS_X, nqy // CORES
    nquad = nz // 2
    nnear, nfar = CHIPS_X * CORES * 2, ny * nquad
    near = (x * CORES + core) * 2 + z % 2
    far = y * nquad + z // 2

    def along_near(s):
        there = lax.rem(near + s, nnear)
        at_x, at_core, at_z = there // (2 * CORES), there // 2 % CORES, z - z % 2 + there % 2
        return there, {"px": y * CHIPS_X + at_x, "qy": at_z * CORES + at_core}

    def along_far(s):
        there = lax.rem(far + s, nfar)
        at_y, at_z = there // nquad, there % nquad * 2 + z % 2
        return there, {"px": at_y * CHIPS_X + x, "qy": at_z * CORES + core}

    loads = []
    pairs = [(x_hbm.at[:, pl.ds(c * 128, 128)], x_in.at[c]) for c in range(TILES)]
    pairs += [(dp_hbm, dp_v), (di_hbm, di_v), (dr_hbm, dr_v), (bd_hbm, bd_v), (sg_hbm, sg_v)]
    pairs += [(rhs_hbm.at[:, pl.ds(c * 128, 128)], rhs_v.at[c]) for c in range(TILES)]
    for n, (src, dst) in enumerate(pairs):
        load = pltpu.make_async_copy(src, dst, in_sem.at[n])
        load.start()
        loads.append(load)

    for edge in (0, 24):
        cx[:, pl.ds(edge, 8), :] = jnp.zeros((3, 8, COLS), F32)
    for edge in (0, ROWS + 1):
        xx[edge] = jnp.zeros((2, 8, WIDE), F32)
    for side in (x_side, f_side, h_side):
        side[...] = jnp.zeros_like(side)
    for t in range(CYCLES):
        for edge in (0, HALO + ROWS):
            p0[t, pl.ds(edge, HALO), :, :, pl.ds(0, COLS)] = jnp.zeros((HALO, 2, 8, COLS), F32)

    def inside(a, b):
        return (px + a >= 0) & (px + a < npx) & (qy + b >= 0) & (qy + b < nqy)

    def device(a, b):
        return {"px": px + a, "qy": qy + b}

    barrier = pltpu.get_barrier_semaphore()
    count = jnp.int32(nnear + nfar - 2)
    for a, b in AROUND:
        count += inside(a, b).astype(jnp.int32)

        @pl.when(inside(a, b))
        def _():
            pl.semaphore_signal(barrier, inc=1, device_id=device(a, b), device_id_type=MESH)

    for along, size in ((along_near, nnear), (along_far, nfar)):
        @pl.loop(1, size)
        def _(s):
            pl.semaphore_signal(barrier, inc=1, device_id=along(s)[1], device_id_type=MESH)

    def start(copies):
        for (a, b), copy in copies:
            pl.when(inside(a, b))(copy.start)

    def arrive(copies):
        for (a, b), copy in copies:
            pl.when(inside(-a, -b))(copy.wait_recv)

    def leave(copies):
        for (a, b), copy in copies:
            pl.when(inside(a, b))(copy.wait_send)

    def remote(src, dst, send, recv, a, b):
        return (a, b), pltpu.make_async_remote_copy(
            src_ref=src, dst_ref=dst, send_sem=send, recv_sem=recv,
            device_id=device(a, b), device_id_type=MESH,
        )

    def edge_copies(out, side, send, recv, corners=True):
        beside, corner = [], []
        for n, (a, b) in enumerate(AROUND):
            if b == 0:
                continue
            s = 0 if b > 0 else 1
            if a == 0:
                beside.append(
                    remote(out, side.at[s, pl.ds(1, 2)], send.at[n], recv.at[n], a, b)
                )
            elif corners:
                from_tile, to_tile = (0, 3) if a < 0 else (1, 0)
                corner.append(
                    remote(out.at[from_tile], side.at[s, to_tile], send.at[n], recv.at[n], a, b)
                )
        return beside, corner

    def both_sides(side, tile):
        lane = lax.broadcasted_iota(jnp.int32, (8, 128), 1)
        return jnp.where(lane % 8 < 4, side[0, tile], side[1, tile])

    for load in loads[:TILES]:
        load.wait()

    def turn(i):
        for c in range(TILES):
            xx[1 + i, :, :, pl.ds(c * 128, 128)] = (
                x_in[c, pl.ds(i, NR, stride=ROWS), :].reshape(2, 8, 128)
            )

    for i in range(ROWS):
        turn(i)

    def pack_rows(ref, first, out):
        for tile in range(2):
            pairs = []
            for i in range(8):
                for h in range(2):
                    row = first + 8 * tile + i
                    pairs.append(
                        edge_pair(ref[row, h, :, pl.ds(0, 128)], ref[row, h, :, pl.ds(COLS - 128, 128)])
                    )
            out[tile] = pack(pairs)

    pack_rows(xx, 1, x_out)
    pl.semaphore_wait(barrier, count)
    x_rows = []
    for a in (-1, 1):
        n = AROUND.index((a, 0))
        x_rows.append(remote(
            xx.at[1 if a < 0 else ROWS, :, :, pl.ds(0, COLS)],
            xx.at[ROWS + 1 if a < 0 else 0, :, :, pl.ds(0, COLS)],
            x_send.at[n], x_recv.at[n], a, 0,
        ))
    x_beside, _ = edge_copies(x_out, x_side, x_send, x_recv, corners=False)
    start(x_beside)
    start(x_rows)

    for load in loads[TILES : TILES + 5]:
        load.wait()
    active = (1 - bd_v[...]).astype(F32)
    upward = sg_v[...].astype(F32)
    price = active * dp_v[...]
    lower = active * (di_v[...] + dr_v[...] * upward)
    higher = active * (di_v[...] + dr_v[...] * (1.0 - upward))
    own = pl.ds(8, ROWS)
    for n, field in enumerate((price, lower, higher)):
        cx[n, own, :] = field
    for tile in range(2):
        rows8 = slice(8 * tile, 8 * tile + 8)
        f_out[tile] = pack([
            edge_pair(field[rows8, :128], field[rows8, COLS - 128 :])
            for field in (price, lower, higher)
        ])
    f_rows = []
    for a in (-1, 1):
        n = AROUND.index((a, 0))
        f_rows.append(remote(
            cx.at[:, pl.ds(8 if a < 0 else 16, 8), :], cx.at[:, pl.ds(24 if a < 0 else 0, 8), :],
            c_send.at[n], c_recv.at[n], a, 0,
        ))
    f_beside, f_corner = edge_copies(f_out, f_side, c_send, c_recv)
    f_copies = f_beside + f_rows + f_corner
    start(f_copies)

    def spread(n, row, value, at, width):
        ce[n, row, :, pl.ds(at, width)] = jnp.broadcast_to(value, (8, width))

    diagonal = 1.0 + 2.0 * price + lower + higher
    for n, field in enumerate((diagonal, price, lower, higher)):
        for i in range(ROWS):
            spread(n, HALO + i, field[i : i + 1], 0, COLS)

    def image_row(above, center, below, row, width):
        def field(n):
            return ce[n, row, :, pl.ds(0, width)][None]

        def cut(value):
            return value[:, :, :width]

        return (
            field(0) * cut(center)
            - field(1) * (cut(above) + cut(below))
            - field(2) * cut(pltpu.roll(center, 1, 2))
            - field(3) * cut(pltpu.roll(center, WIDE - 1, 2))
        )

    for load in loads[TILES + 5 :]:
        load.wait()
    arrive(x_beside)
    for i in range(ROWS):
        tile = both_sides(x_side, 1 + i // 8)
        for h in range(2):
            xx[1 + i, h, :, pl.ds(COLS, 128)] = unpack(tile, 2 * (i % 8) + h)
    arrive(x_rows)

    def first_residual(i):
        value = image_row(xx[i], xx[1 + i], xx[2 + i], HALO + i, COLS)
        for c in range(TILES):
            p0[0, HALO + i, :, :, pl.ds(c * 128, 128)] = (
                rhs_v[c, pl.ds(i, NR, stride=ROWS), :].reshape(2, 8, 128)
                - value[:, :, c * 128 : c * 128 + 128]
            )

    def rim_rows(t):
        copies = []
        for a in (-1, 1):
            n = AROUND.index((a, 0))
            copies.append(remote(
                p0.at[t, pl.ds(HALO if a < 0 else ROWS, HALO), :, :, pl.ds(0, COLS)],
                p0.at[t, pl.ds(HALO + ROWS if a < 0 else 0, HALO), :, :, pl.ds(0, COLS)],
                h_send.at[t, n], h_recv.at[t, n], a, 0,
            ))
        return copies

    def outer_rows_first(body, t):
        for begin in (0, ROWS - HALO):
            for i in range(begin, begin + HALO):
                body(i)
        if t < CYCLES:
            start(rim_rows(t))
        for i in range(HALO, ROWS - HALO):
            body(i)

    outer_rows_first(first_residual, 0)

    def total(t, local):
        for j in range(nnear):
            rs_out[j] = local[2 * j : 2 * j + 2]
        rs_buf[t, near] = rs_out[near]

        def phase(n, along, size, src, buf, me):
            steps = [s for d in range(size // 2, 0, -1) for s in sorted({d, size - d})]
            for s in steps:
                there, where = along(s)
                pltpu.make_async_remote_copy(
                    src_ref=src(there), dst_ref=buf.at[t, me],
                    send_sem=sum_send.at[n], recv_sem=sum_recv.at[t, n],
                    device_id=where, device_id_type=MESH,
                ).start()
            whole = pltpu.make_async_remote_copy(
                src_ref=buf.at[t, pl.ds(0, size - 1)], dst_ref=buf.at[t, pl.ds(0, size - 1)],
                send_sem=sum_send.at[n], recv_sem=sum_recv.at[t, n],
                device_id={"px": px, "qy": qy}, device_id_type=MESH,
            )
            whole.wait_recv()
            return whole

        sent = [phase(0, along_near, nnear, lambda there: rs_out.at[there], rs_buf, near)]
        as_buf[t, far] = jnp.sum(rs_buf[t], axis=0)
        sent.append(phase(1, along_far, nfar, lambda there: as_buf.at[t, far], as_buf, far))
        ag_buf[t, near] = jnp.sum(as_buf[t], axis=0)
        sent.append(phase(2, along_near, nnear, lambda there: ag_buf.at[t, near], ag_buf, near))
        for j in range(nnear):
            packed_v[pl.ds(2 * j, 2), :] = ag_buf[t, j]
        return packed_v[...], sent

    def solve(both):
        tiles = [both[8 * r : 8 * r + 8] for r in range(8)]
        at = lax.broadcasted_iota(jnp.int32, (8, 128), 0)

        def across(row):
            return jnp.broadcast_to(row, (8, 128))

        for b in range(8):
            columns = [
                [jnp.broadcast_to(tile[:, n : n + 1], (8, 128)) for tile in tiles]
                for n in range(8 * b, 8 * b + 8)
            ]
            for j in range(8):
                pivots = columns[j]
                inverse = 1.0 / across(pivots[b][j : j + 1])

                def eliminate(group):
                    row = across(group[b][j : j + 1]) * inverse
                    after = [g - c * row for g, c in zip(group, pivots)]
                    after[b] = jnp.where(at == j, row, after[b])
                    return after

                for q in range(j + 1, 8):
                    columns[q] = eliminate(columns[q])
                tiles = eliminate(tiles)
        return jnp.concatenate(tiles, axis=0)

    def keep_limbs(i, block, value):
        for n, limb in enumerate(limbs(value[:, :, :COLS].reshape(NR, COLS))):
            basis[i, pl.ds(n * BASIS + block * NR, NR), :] = limb

    for t in range(CYCLES):
        last = t == CYCLES - 1
        fields = [p0.at[t], p1, p2, p3]
        rims = rim_rows(t)
        pack_rows(p0.at[t], HALO, h_out.at[t])
        beside, corner = edge_copies(h_out.at[t], h_side.at[t], h_send.at[t], h_recv.at[t])
        start(beside)
        start(corner)

        for i in range(ROWS):
            keep_limbs(i, STEPS, p0[t, HALO + i])

        if t == 0:
            arrive(f_copies)
            for p in range(EXT):
                row = 8 - HALO + p
                tile = both_sides(f_side, row // 8)
                values = [unpack(tile, n)[row % 8 : row % 8 + 1] for n in range(3)]
                values = [1.0 + 2.0 * values[0] + values[1] + values[2]] + values
                for n, value in enumerate(values):
                    spread(n, p, value, COLS, 128)
                if HALO <= p < HALO + ROWS:
                    continue
                values = [cx[n, pl.ds(row, 1), :] for n in range(3)]
                values = [1.0 + 2.0 * values[0] + values[1] + values[2]] + values
                for n, value in enumerate(values):
                    spread(n, p, value, 0, COLS)

        def lanes_around(p):
            row = 8 - HALO + p
            tile = both_sides(h_side.at[t], row // 8)
            for h in range(2):
                p0[t, p, h, :, pl.ds(COLS, 128)] = unpack(tile, 2 * (row % 8) + h)

        def advance(k, rows, inner):
            for p, own_row in zip(rows, inner):
                center = fields[k][p]
                image = image_row(
                    fields[k][p - 1], center, fields[k][p + 1], p,
                    WIDE if k < STEPS - 1 else COLS,
                )
                if k < STEPS - 1:
                    fields[k + 1][p] = image * (1.0 / THETA) - center * (SIGMA / THETA)
                if own_row:
                    keep_limbs(p - HALO, k, image)

        arrive(beside)
        for p in range(HALO, HALO + ROWS):
            lanes_around(p)
        for k in range(STEPS):
            rows = range(HALO + 1 + k, HALO + ROWS - 1 - k)
            advance(k, rows, [True] * len(rows))

        def gram_step(i, acc):
            for n in range(4):
                part = basis[4 * i + n]
                acc = acc + lax.dot_general(
                    part, part, (((1,), (1,)), ((), ())), preferred_element_type=F32
                )
            return acc

        acc = gram_step(2, gram_step(1, jnp.zeros((3 * BASIS, 3 * BASIS), F32)))

        arrive(rims)
        arrive(corner)
        for begin in (0, HALO + ROWS):
            for p in range(begin, begin + HALO):
                lanes_around(p)
        for k in range(STEPS):
            for begin in (k + 1, EXT - 5 - k):
                rows = [begin + n for n in range(4)]
                inner = [HALO <= p < HALO + ROWS for p in rows]
                advance(k, rows, inner)

        acc = gram_step(3, gram_step(0, acc))
        rows = acc[2 * BASIS :] + acc[BASIS : 2 * BASIS] + acc[:BASIS]
        gram = rows[:64, 2 * BASIS :] + rows[:64, BASIS : 2 * BASIS] + rows[:64, :BASIS]
        gram = jnp.concatenate([gram, jnp.zeros((64, 48), F32)], axis=1)
        lane = lax.broadcasted_iota(jnp.int32, (32, 128), 1)
        packed = jnp.where(lane < 80, gram[:32], pltpu.roll(gram[32:], 48, 1))
        packed, sent = total(t, packed)
        lower = pltpu.roll(packed, 80, 1)
        square = jnp.concatenate([packed, jnp.zeros((96, 128), F32)], axis=0)
        turned = square.T
        lower = jnp.where(lane < 32, turned[32:64], lower)
        answer = solve(jnp.concatenate([packed, lower], axis=0))
        if t == 0:
            leave(x_beside + x_rows + f_copies)
        leave(rims + beside + corner)
        for whole in sent:
            whole.wait_send()

        u = [answer[NR * k : NR * (k + 1)] for k in range(STEPS)]
        e = [None] * STEPS
        e[STEPS - 1] = u[STEPS - 1]
        for k in range(STEPS - 2, -1, -1):
            e[k] = u[k] - (SIGMA / THETA) * e[k + 1]
        lane = lax.broadcasted_iota(jnp.int32, (NR, 128), 1)
        blocks = []
        for k in range(STEPS + 1):
            to_res = -u[k] if k < STEPS else jnp.zeros_like(u[0])
            if k == STEPS:
                to_sol = e[0]
            elif k < STEPS - 1:
                to_sol = e[k + 1] * (1.0 / THETA)
            else:
                to_sol = jnp.zeros_like(u[0])
            blocks.append(jnp.where(lane < 80, to_res, pltpu.roll(to_sol, NR, 1)))
        blocks.append(jnp.zeros((48, 128), F32))
        weights = jnp.concatenate(blocks, axis=0).T[64:96, :BASIS]
        high, mid, low = limbs(weights)
        three = jnp.concatenate([high, mid, low], axis=0)
        three = jnp.concatenate([three] * 3, axis=1)

        def update(i):
            parts = jnp.dot(three, basis[i], preferred_element_type=F32)
            change = (parts[64:] + parts[32:64]) + parts[:32]
            res = p0[t, HALO + i, :, :, pl.ds(0, COLS)] + change[:NR].reshape(2, 8, COLS)
            sol = xx[1 + i, :, :, pl.ds(0, COLS)] + change[NR:].reshape(2, 8, COLS)
            if last:
                for c in range(TILES):
                    part = slice(c * 128, c * 128 + 128)
                    rhs_v[c, pl.ds(i, NR, stride=ROWS), :] = res[:, :, part].reshape(NR, 128)
                    x_in[c, pl.ds(i, NR, stride=ROWS), :] = sol[:, :, part].reshape(NR, 128)
            else:
                p0[t + 1, HALO + i, :, :, pl.ds(0, COLS)] = res
                xx[1 + i, :, :, pl.ds(0, COLS)] = sol

        outer_rows_first(update, t + 1)

    stores = []
    for src, dst in ((x_in, sol_hbm), (rhs_v, res_hbm)):
        for c in range(TILES):
            store = pltpu.make_async_copy(
                src.at[c], dst.at[:, pl.ds(c * 128, 128)], in_sem.at[len(stores)]
            )
            store.start()
            stores.append(store)
    for store in stores:
        store.wait()


def solution(mesh):
    npx, nqy = mesh.shape["px"], mesh.shape["qy"]

    def per_device(rhs, iterate, *fields):
        flat = jax.ShapeDtypeStruct((NR * ROWS, COLS), F32)
        vmem = pltpu.VMEM
        dma = pltpu.SemaphoreType.DMA
        field = vmem((EXT, 2, 8, WIDE), F32)
        plane = vmem((ROWS, COLS), F32)
        marks = vmem((ROWS, COLS), jnp.int32)
        turned = vmem((TILES, NR * ROWS, 128), F32)
        sixteenth = vmem((CYCLES, 16, 2, 128), F32)
        sol, res = pl.pallas_call(
            lambda *refs: kernel(npx, nqy, *refs),
            out_shape=(flat, flat),
            in_specs=[pl.BlockSpec(memory_space=pl.ANY)] * 7,
            out_specs=(pl.BlockSpec(memory_space=pl.ANY),) * 2,
            scratch_shapes=[
                turned, turned, plane, plane, plane, marks, marks,
                vmem((3, ROWS + 16, COLS), F32),
                vmem((4, EXT, 8, WIDE), F32),
                vmem((ROWS + 2, 2, 8, WIDE), F32),
                vmem((CYCLES, EXT, 2, 8, WIDE), F32),
                field, field, field,
                vmem((ROWS, 3 * BASIS, COLS), BF16),
                vmem((2, 8, 128), F32), vmem((2, 4, 8, 128), F32),
                vmem((2, 8, 128), F32), vmem((2, 4, 8, 128), F32),
                vmem((CYCLES, 2, 8, 128), F32), vmem((CYCLES, 2, 4, 8, 128), F32),
                vmem((16, 2, 128), F32), sixteenth, vmem((CYCLES, 32, 2, 128), F32), sixteenth,
                vmem((32, 128), F32),
                dma((5 + 2 * TILES,)),
                dma((8,)), dma((8,)), dma((8,)), dma((8,)),
                dma((CYCLES, 8)), dma((CYCLES, 8)),
                dma((3,)), dma((CYCLES, 3)),
            ],
            compiler_params=pltpu.CompilerParams(
                collective_id=0, has_side_effects=True, vmem_limit_bytes=62 * 1024 * 1024
            ),
        )(rhs.reshape(NR * ROWS, COLS), iterate.reshape(NR * ROWS, COLS), *fields)
        return sol.reshape(NR, ROWS, COLS), res.reshape(NR, ROWS, COLS)

    whole, plane = P(None, "px", "qy"), P("px", "qy")
    return jax.shard_map(
        per_device, mesh=mesh, in_specs=(whole, whole) + (plane,) * 5,
        out_specs=(whole, whole), check_vma=False,
    )
```

```python
import jax
import jax.numpy as jnp
from jax import lax
from jax.experimental import pallas as pl
from jax.experimental.pallas import tpu as pltpu
from jax.sharding import PartitionSpec as P

STEPS = 4
CYCLES = 2
SIGMA = 5.5
THETA = 4.5
HALO = STEPS
NR = 16
ROWS = 16
COLS = 512
TILES = COLS // 128
WIDE = COLS + 128
EXT = ROWS + 2 * HALO
BASIS = NR * (STEPS + 1)
CORES = 2
CHIPS_X = 4
MESH = pl.DeviceIdType.MESH
F32 = jnp.float32
BF16 = jnp.bfloat16
AROUND = [(a, b) for a in (-1, 0, 1) for b in (-1, 0, 1) if (a, b) != (0, 0)]


def limbs(x):
    high = x.astype(BF16)
    rest = x - high.astype(F32)
    mid = rest.astype(BF16)
    low = (rest - mid.astype(F32)).astype(BF16)
    return high, mid, low


def lanes_of(x):
    return lax.broadcasted_iota(jnp.int32, x.shape, x.ndim - 1)


def edge_pair(first, last):
    return jnp.where(lanes_of(first) < 64, first, last)


def pack(pairs):
    packed = jnp.zeros_like(pairs[0])
    lane = lanes_of(packed)
    for n, pair in enumerate(pairs):
        packed = jnp.where(lane // 8 == n, pltpu.roll(pair, (8 * n + 4) % 128, 1), packed)
    return packed


def unpack(packed, n):
    return pltpu.roll(packed, (124 - 8 * n) % 128, 1)


def kernel(
    npx, nqy,
    rhs_hbm, x_hbm, dp_hbm, di_hbm, dr_hbm, bd_hbm, sg_hbm,
    basis, sol_out, res_out, weights_out,
    rhs_v, x_in, dp_v, di_v, dr_v, bd_v, sg_v,
    cx, ce, xx, p0, p1, p2, p3,
    x_out, x_side, f_out, f_side, h_out, h_side,
    rs_out, rs_buf, as_buf, ag_buf, packed_v,
    in_sem, c_send, c_recv, x_send, x_recv, h_send, h_recv,
    sum_send, sum_recv,
):
    px, qy = lax.axis_index("px"), lax.axis_index("qy")
    y, x = px // CHIPS_X, px % CHIPS_X
    z, core = qy // CORES, qy % CORES
    ny, nz = npx // CHIPS_X, nqy // CORES
    nquad = nz // 2
    nnear, nfar = CHIPS_X * CORES * 2, ny * nquad
    near = (x * CORES + core) * 2 + z % 2
    far = y * nquad + z // 2

    def along_near(s):
        there = lax.rem(near + s, nnear)
        at_x, at_core, at_z = there // (2 * CORES), there // 2 % CORES, z - z % 2 + there % 2
        return there, {"px": y * CHIPS_X + at_x, "qy": at_z * CORES + at_core}

    def along_far(s):
        there = lax.rem(far + s, nfar)
        at_y, at_z = there // nquad, there % nquad * 2 + z % 2
        return there, {"px": at_y * CHIPS_X + x, "qy": at_z * CORES + core}

    def inside(a, b):
        return (px + a >= 0) & (px + a < npx) & (qy + b >= 0) & (qy + b < nqy)

    def device(a, b):
        return {"px": px + a, "qy": qy + b}

    barrier = pltpu.get_barrier_semaphore()
    count = jnp.int32(nnear + nfar - 2)
    for a, b in AROUND:
        count += inside(a, b).astype(jnp.int32)

        @pl.when(inside(a, b))
        def _():
            pl.semaphore_signal(barrier, inc=1, device_id=device(a, b), device_id_type=MESH)

    loads = []
    pairs = [(x_hbm.at[:, pl.ds(c * 128, 128)], x_in.at[c]) for c in range(TILES)]
    pairs += [(dp_hbm, dp_v), (di_hbm, di_v), (dr_hbm, dr_v), (bd_hbm, bd_v), (sg_hbm, sg_v)]
    pairs += [(rhs_hbm.at[:, pl.ds(c * 128, 128)], rhs_v.at[c]) for c in range(TILES)]
    for n, (src, dst) in enumerate(pairs):
        load = pltpu.make_async_copy(src, dst, in_sem.at[n])
        load.start()
        loads.append(load)

    for along, size in ((along_near, nnear), (along_far, nfar)):
        @pl.loop(1, size)
        def _(s):
            pl.semaphore_signal(barrier, inc=1, device_id=along(s)[1], device_id_type=MESH)

    for a, b in AROUND:
        @pl.when(jnp.logical_not(inside(a, b)))
        def _():
            if b == 0:
                edge = 0 if a < 0 else 24
                cx[:, pl.ds(edge, 8), :] = jnp.zeros((3, 8, COLS), F32)
                edge = 0 if a < 0 else ROWS + 1
                xx[edge, :, :, pl.ds(0, COLS)] = jnp.zeros((2, 8, COLS), F32)
                edge = 0 if a < 0 else HALO + ROWS
                for t in range(CYCLES):
                    p0[t, pl.ds(edge, HALO), :, :, pl.ds(0, COLS)] = (
                        jnp.zeros((HALO, 2, 8, COLS), F32)
                    )
                return
            s = 0 if b < 0 else 1
            tiles = {-1: (0,), 0: (1, 2), 1: (3,)}[a]
            for n in tiles:
                if a == 0:
                    x_side[s, n] = jnp.zeros((8, 128), F32)
                f_side[s, n] = jnp.zeros((8, 128), F32)
                for t in range(CYCLES):
                    h_side[t, s, n] = jnp.zeros((8, 128), F32)

    def start(copies):
        for (a, b), copy in copies:
            pl.when(inside(a, b))(copy.start)

    def arrive(copies):
        for (a, b), copy in copies:
            pl.when(inside(-a, -b))(copy.wait_recv)

    def leave(copies):
        for (a, b), copy in copies:
            pl.when(inside(a, b))(copy.wait_send)

    def remote(src, dst, send, recv, a, b):
        return (a, b), pltpu.make_async_remote_copy(
            src_ref=src, dst_ref=dst, send_sem=send, recv_sem=recv,
            device_id=device(a, b), device_id_type=MESH,
        )

    def edge_copies(out, side, send, recv, corners=True):
        beside, corner = [], []
        for n, (a, b) in enumerate(AROUND):
            if b == 0:
                continue
            s = 0 if b > 0 else 1
            if a == 0:
                beside.append(
                    remote(out, side.at[s, pl.ds(1, 2)], send.at[n], recv.at[n], a, b)
                )
            elif corners:
                from_tile, to_tile = (0, 3) if a < 0 else (1, 0)
                corner.append(
                    remote(out.at[from_tile], side.at[s, to_tile], send.at[n], recv.at[n], a, b)
                )
        return beside, corner

    def both_sides(side, tile):
        lane = lax.broadcasted_iota(jnp.int32, (8, 128), 1)
        return jnp.where(lane % 8 < 4, side[0, tile], side[1, tile])

    for load in loads[:TILES]:
        load.wait()

    def turn(i):
        for c in range(TILES):
            xx[1 + i, :, :, pl.ds(c * 128, 128)] = (
                x_in[c, pl.ds(i, NR, stride=ROWS), :].reshape(2, 8, 128)
            )

    for i in range(ROWS):
        turn(i)

    def pack_rows(ref, first, out):
        for tile in range(2):
            pairs = []
            for i in range(8):
                for h in range(2):
                    row = first + 8 * tile + i
                    pairs.append(
                        edge_pair(ref[row, h, :, pl.ds(0, 128)], ref[row, h, :, pl.ds(COLS - 128, 128)])
                    )
            out[tile] = pack(pairs)

    pack_rows(xx, 1, x_out)
    pl.semaphore_wait(barrier, count)
    x_rows = []
    for a in (-1, 1):
        n = AROUND.index((a, 0))
        x_rows.append(remote(
            xx.at[1 if a < 0 else ROWS, :, :, pl.ds(0, COLS)],
            xx.at[ROWS + 1 if a < 0 else 0, :, :, pl.ds(0, COLS)],
            x_send.at[n], x_recv.at[n], a, 0,
        ))
    x_beside, _ = edge_copies(x_out, x_side, x_send, x_recv, corners=False)
    start(x_beside)
    start(x_rows)

    for load in loads[TILES : TILES + 5]:
        load.wait()
    active = (1 - bd_v[...]).astype(F32)
    upward = sg_v[...].astype(F32)
    price = active * dp_v[...]
    lower = active * (di_v[...] + dr_v[...] * upward)
    higher = active * (di_v[...] + dr_v[...] * (1.0 - upward))
    own = pl.ds(8, ROWS)
    for n, field in enumerate((price, lower, higher)):
        cx[n, own, :] = field
    for tile in range(2):
        rows8 = slice(8 * tile, 8 * tile + 8)
        f_out[tile] = pack([
            edge_pair(field[rows8, :128], field[rows8, COLS - 128 :])
            for field in (price, lower, higher)
        ])
    f_rows = []
    for a in (-1, 1):
        n = AROUND.index((a, 0))
        f_rows.append(remote(
            cx.at[:, pl.ds(8 if a < 0 else 16, 8), :], cx.at[:, pl.ds(24 if a < 0 else 0, 8), :],
            c_send.at[n], c_recv.at[n], a, 0,
        ))
    f_beside, f_corner = edge_copies(f_out, f_side, c_send, c_recv)
    f_copies = f_beside + f_rows + f_corner
    start(f_copies)

    def spread(n, row, value, at, width):
        ce[n, row, :, pl.ds(at, width)] = jnp.broadcast_to(value, (8, width))

    diagonal = 1.0 + 2.0 * price + lower + higher
    for n, field in enumerate((diagonal, price, lower, higher)):
        for i in range(ROWS):
            spread(n, HALO + i, field[i : i + 1], 0, COLS)

    def image_row(above, center, below, row, width):
        def field(n):
            return ce[n, row, :, pl.ds(0, width)][None]

        def cut(value):
            return value[:, :, :width]

        return (
            field(0) * cut(center)
            - field(1) * (cut(above) + cut(below))
            - field(2) * cut(pltpu.roll(center, 1, 2))
            - field(3) * cut(pltpu.roll(center, WIDE - 1, 2))
        )

    for load in loads[TILES + 5 :]:
        load.wait()
    arrive(x_beside)
    for i in range(ROWS):
        tile = both_sides(x_side, 1 + i // 8)
        for h in range(2):
            xx[1 + i, h, :, pl.ds(COLS, 128)] = unpack(tile, 2 * (i % 8) + h)
    arrive(x_rows)

    def first_residual(i):
        value = image_row(xx[i], xx[1 + i], xx[2 + i], HALO + i, COLS)
        for c in range(TILES):
            p0[0, HALO + i, :, :, pl.ds(c * 128, 128)] = (
                rhs_v[c, pl.ds(i, NR, stride=ROWS), :].reshape(2, 8, 128)
                - value[:, :, c * 128 : c * 128 + 128]
            )

    def rim_rows(t):
        copies = []
        for a in (-1, 1):
            n = AROUND.index((a, 0))
            copies.append(remote(
                p0.at[t, pl.ds(HALO if a < 0 else ROWS, HALO), :, :, pl.ds(0, COLS)],
                p0.at[t, pl.ds(HALO + ROWS if a < 0 else 0, HALO), :, :, pl.ds(0, COLS)],
                h_send.at[t, n], h_recv.at[t, n], a, 0,
            ))
        return copies

    def outer_rows_first(body, t):
        for begin in (0, ROWS - HALO):
            for i in range(begin, begin + HALO):
                body(i)
        if t < CYCLES:
            start(rim_rows(t))
        for i in range(HALO, ROWS - HALO):
            body(i)

    outer_rows_first(first_residual, 0)

    def total(t, local):
        for j in range(nnear):
            rs_out[j] = local[2 * j : 2 * j + 2]
        rs_buf[t, near] = rs_out[near]

        def phase(n, along, size, src, buf, me):
            steps = [s for d in range(size // 2, 0, -1) for s in sorted({d, size - d})]
            for s in steps:
                there, where = along(s)
                pltpu.make_async_remote_copy(
                    src_ref=src(there), dst_ref=buf.at[t, me],
                    send_sem=sum_send.at[n], recv_sem=sum_recv.at[t, n],
                    device_id=where, device_id_type=MESH,
                ).start()
            whole = pltpu.make_async_remote_copy(
                src_ref=buf.at[t, pl.ds(0, size - 1)], dst_ref=buf.at[t, pl.ds(0, size - 1)],
                send_sem=sum_send.at[n], recv_sem=sum_recv.at[t, n],
                device_id={"px": px, "qy": qy}, device_id_type=MESH,
            )
            whole.wait_recv()
            return whole

        sent = [phase(0, along_near, nnear, lambda there: rs_out.at[there], rs_buf, near)]
        as_buf[t, far] = jnp.sum(rs_buf[t], axis=0)
        sent.append(phase(1, along_far, nfar, lambda there: as_buf.at[t, far], as_buf, far))
        ag_buf[t, near] = jnp.sum(as_buf[t], axis=0)
        sent.append(phase(2, along_near, nnear, lambda there: ag_buf.at[t, near], ag_buf, near))
        for j in range(nnear):
            packed_v[pl.ds(2 * j, 2), :] = ag_buf[t, j]
        return packed_v[...], sent

    def solve(both):
        tiles = [both[8 * r : 8 * r + 8] for r in range(8)]
        at = lax.broadcasted_iota(jnp.int32, (8, 128), 0)

        def across(row):
            return jnp.broadcast_to(row, (8, 128))

        for b in range(8):
            columns = [
                [jnp.broadcast_to(tile[:, n : n + 1], (8, 128)) for tile in tiles]
                for n in range(8 * b, 8 * b + 8)
            ]
            for j in range(8):
                pivots = columns[j]
                inverse = 1.0 / across(pivots[b][j : j + 1])

                def eliminate(group):
                    row = across(group[b][j : j + 1]) * inverse
                    after = [g - c * row for g, c in zip(group, pivots)]
                    after[b] = jnp.where(at == j, row, after[b])
                    return after

                for q in range(j + 1, 8):
                    columns[q] = eliminate(columns[q])
                tiles = eliminate(tiles)
        return jnp.concatenate(tiles, axis=0)

    def keep_limbs(i, block, value):
        for n, limb in enumerate(limbs(value[:, :, :COLS].reshape(NR, COLS))):
            basis[i, pl.ds(n * BASIS + block * NR, NR), :] = limb

    for t in range(CYCLES):
        last = t == CYCLES - 1
        fields = [p0.at[t], p1, p2, p3]
        rims = rim_rows(t)
        pack_rows(p0.at[t], HALO, h_out.at[t])
        beside, corner = edge_copies(h_out.at[t], h_side.at[t], h_send.at[t], h_recv.at[t])
        start(beside)
        start(corner)

        for i in range(ROWS):
            keep_limbs(i, STEPS, p0[t, HALO + i])

        if t == 0:
            arrive(f_copies)
            for p in range(EXT):
                row = 8 - HALO + p
                tile = both_sides(f_side, row // 8)
                values = [unpack(tile, n)[row % 8 : row % 8 + 1] for n in range(3)]
                values = [1.0 + 2.0 * values[0] + values[1] + values[2]] + values
                for n, value in enumerate(values):
                    spread(n, p, value, COLS, 128)
                if HALO <= p < HALO + ROWS:
                    continue
                values = [cx[n, pl.ds(row, 1), :] for n in range(3)]
                values = [1.0 + 2.0 * values[0] + values[1] + values[2]] + values
                for n, value in enumerate(values):
                    spread(n, p, value, 0, COLS)

        def lanes_around(p):
            row = 8 - HALO + p
            tile = both_sides(h_side.at[t], row // 8)
            for h in range(2):
                p0[t, p, h, :, pl.ds(COLS, 128)] = unpack(tile, 2 * (row % 8) + h)

        def advance(k, rows, inner):
            for p, own_row in zip(rows, inner):
                center = fields[k][p]
                image = image_row(
                    fields[k][p - 1], center, fields[k][p + 1], p,
                    WIDE if k < STEPS - 1 else COLS,
                )
                if k < STEPS - 1:
                    fields[k + 1][p] = image * (1.0 / THETA) - center * (SIGMA / THETA)
                if own_row:
                    keep_limbs(p - HALO, k, image)

        arrive(beside)
        for p in range(HALO, HALO + ROWS):
            lanes_around(p)
        for k in range(STEPS):
            rows = range(HALO + 1 + k, HALO + ROWS - 1 - k)
            advance(k, rows, [True] * len(rows))

        def gram_step(i, acc):
            for n in range(4):
                part = basis[4 * i + n]
                acc = acc + lax.dot_general(
                    part, part, (((1,), (1,)), ((), ())), preferred_element_type=F32
                )
            return acc

        acc = gram_step(2, gram_step(1, jnp.zeros((3 * BASIS, 3 * BASIS), F32)))

        arrive(rims)
        arrive(corner)
        for begin in (0, HALO + ROWS):
            for p in range(begin, begin + HALO):
                lanes_around(p)
        for k in range(STEPS):
            for begin in (k + 1, EXT - 5 - k):
                rows = [begin + n for n in range(4)]
                inner = [HALO <= p < HALO + ROWS for p in rows]
                advance(k, rows, inner)

        acc = gram_step(3, gram_step(0, acc))
        rows = acc[2 * BASIS :] + acc[BASIS : 2 * BASIS] + acc[:BASIS]
        gram = rows[:64, 2 * BASIS :] + rows[:64, BASIS : 2 * BASIS] + rows[:64, :BASIS]
        gram = jnp.concatenate([gram, jnp.zeros((64, 48), F32)], axis=1)
        lane = lax.broadcasted_iota(jnp.int32, (32, 128), 1)
        packed = jnp.where(lane < 80, gram[:32], pltpu.roll(gram[32:], 48, 1))
        packed, sent = total(t, packed)
        lower = pltpu.roll(packed, 80, 1)
        square = jnp.concatenate([packed, jnp.zeros((96, 128), F32)], axis=0)
        turned = square.T
        lower = jnp.where(lane < 32, turned[32:64], lower)
        answer = solve(jnp.concatenate([packed, lower], axis=0))
        if t == 0:
            leave(x_beside + x_rows + f_copies)
        leave(rims + beside + corner)
        for whole in sent:
            whole.wait_send()

        u = [answer[NR * k : NR * (k + 1)] for k in range(STEPS)]
        e = [None] * STEPS
        e[STEPS - 1] = u[STEPS - 1]
        for k in range(STEPS - 2, -1, -1):
            e[k] = u[k] - (SIGMA / THETA) * e[k + 1]
        lane = lax.broadcasted_iota(jnp.int32, (NR, 128), 1)
        blocks = []
        for k in range(STEPS + 1):
            to_res = -u[k] if k < STEPS else jnp.zeros_like(u[0])
            if k == STEPS:
                to_sol = e[0]
            elif k < STEPS - 1:
                to_sol = e[k + 1] * (1.0 / THETA)
            else:
                to_sol = jnp.zeros_like(u[0])
            blocks.append(jnp.where(lane < 80, to_res, pltpu.roll(to_sol, NR, 1)))
        blocks.append(jnp.zeros((48, 128), F32))
        weights = jnp.concatenate(blocks, axis=0).T[64:96, :BASIS]
        high, mid, low = limbs(weights)
        three = jnp.concatenate([high, mid, low], axis=0)
        three = jnp.concatenate([three] * 3, axis=1)

        if last:
            weights_out[...] = three
            break

        def update(i):
            change = combined(three, basis[i])
            res = p0[t, HALO + i, :, :, pl.ds(0, COLS)] + change[0]
            p0[t + 1, HALO + i, :, :, pl.ds(0, COLS)] = res
            res_out[i] = res
            sol_out[i] = xx[1 + i, :, :, pl.ds(0, COLS)] + change[1]

        outer_rows_first(update, t + 1)


def combined(weights, rows):
    parts = jnp.dot(weights, rows, preferred_element_type=F32)
    change = (parts[64:] + parts[32:64]) + parts[:32]
    return change[:NR].reshape(2, 8, COLS), change[NR:].reshape(2, 8, COLS)


def finish(basis, sol_in, res_in, weights, sol_hbm, res_hbm, sol_v, res_v, sem):
    for i in range(ROWS):
        change = combined(weights[...], basis[i])
        res, sol = res_in[i] + change[0], sol_in[i] + change[1]
        for c in range(TILES):
            part = slice(c * 128, c * 128 + 128)
            res_v[c, pl.ds(i, NR, stride=ROWS), :] = res[:, :, part].reshape(NR, 128)
            sol_v[c, pl.ds(i, NR, stride=ROWS), :] = sol[:, :, part].reshape(NR, 128)
    stores = []
    for src, dst in ((sol_v, sol_hbm), (res_v, res_hbm)):
        for c in range(TILES):
            store = pltpu.make_async_copy(
                src.at[c], dst.at[:, pl.ds(c * 128, 128)], sem.at[len(stores)]
            )
            store.start()
            stores.append(store)
    for store in stores:
        store.wait()


def solution(mesh):
    npx, nqy = mesh.shape["px"], mesh.shape["qy"]

    def per_device(rhs, iterate, *fields):
        flat = jax.ShapeDtypeStruct((NR * ROWS, COLS), F32)
        vmem = pltpu.VMEM
        dma = pltpu.SemaphoreType.DMA
        field = vmem((EXT, 2, 8, WIDE), F32)
        plane = vmem((ROWS, COLS), F32)
        marks = vmem((ROWS, COLS), jnp.int32)
        turned = vmem((TILES, NR * ROWS, 128), F32)
        sixteenth = vmem((CYCLES, 16, 2, 128), F32)
        held = jax.ShapeDtypeStruct((ROWS, 2, 8, COLS), F32)
        parts = pl.pallas_call(
            lambda *refs: kernel(npx, nqy, *refs),
            out_shape=(
                jax.ShapeDtypeStruct((ROWS, 3 * BASIS, COLS), BF16), held, held,
                jax.ShapeDtypeStruct((96, 3 * BASIS), BF16),
            ),
            in_specs=[pl.BlockSpec(memory_space=pl.ANY)] * 7,
            out_specs=(pl.BlockSpec(memory_space=vmem),) * 4,
            scratch_shapes=[
                turned, turned, plane, plane, plane, marks, marks,
                vmem((3, ROWS + 16, COLS), F32),
                vmem((4, EXT, 8, WIDE), F32),
                vmem((ROWS + 2, 2, 8, WIDE), F32),
                vmem((CYCLES, EXT, 2, 8, WIDE), F32),
                field, field, field,
                vmem((2, 8, 128), F32), vmem((2, 4, 8, 128), F32),
                vmem((2, 8, 128), F32), vmem((2, 4, 8, 128), F32),
                vmem((CYCLES, 2, 8, 128), F32), vmem((CYCLES, 2, 4, 8, 128), F32),
                vmem((16, 2, 128), F32), sixteenth, vmem((CYCLES, 32, 2, 128), F32), sixteenth,
                vmem((32, 128), F32),
                dma((5 + 2 * TILES,)),
                dma((8,)), dma((8,)), dma((8,)), dma((8,)),
                dma((CYCLES, 8)), dma((CYCLES, 8)),
                dma((3,)), dma((CYCLES, 3)),
            ],
            compiler_params=pltpu.CompilerParams(
                collective_id=0, has_side_effects=True, vmem_limit_bytes=48 * 1024 * 1024
            ),
        )(*[
            pltpu.with_memory_space_constraint(a, pltpu.HBM) for a in
            (rhs.reshape(NR * ROWS, COLS), iterate.reshape(NR * ROWS, COLS)) + fields
        ])
        sol, res = pl.pallas_call(
            finish,
            out_shape=(flat, flat),
            in_specs=[pl.BlockSpec(memory_space=vmem)] * 4,
            out_specs=(pl.BlockSpec(memory_space=pl.ANY),) * 2,
            scratch_shapes=[turned, turned, dma((2 * TILES,))],
            compiler_params=pltpu.CompilerParams(vmem_limit_bytes=48 * 1024 * 1024),
        )(*parts)
        return sol.reshape(NR, ROWS, COLS), res.reshape(NR, ROWS, COLS)

    whole, plane = P(None, "px", "qy"), P("px", "qy")
    return jax.shard_map(
        per_device, mesh=mesh, in_specs=(whole, whole) + (plane,) * 5,
        out_specs=(whole, whole), check_vma=False,
    )
```

```python
import jax
import jax.numpy as jnp
from jax import lax
from jax.experimental import pallas as pl
from jax.experimental.pallas import tpu as pltpu
from jax.sharding import PartitionSpec as P

STEPS = 4
CYCLES = 2
SIGMA = 5.5
THETA = 4.5
HALO = STEPS
PIECES = 4
NR = 16
ROWS = 16
COLS = 512
TILES = COLS // 128
WIDE = COLS + 128
EXT = ROWS + 2 * HALO
BASIS = NR * (STEPS + 1)
CORES = 2
CHIPS_X = 4
MESH = pl.DeviceIdType.MESH
F32 = jnp.float32
BF16 = jnp.bfloat16
AROUND = [(a, b) for a in (-1, 0, 1) for b in (-1, 0, 1) if (a, b) != (0, 0)]


def limbs(x):
    high = x.astype(BF16)
    rest = x - high.astype(F32)
    mid = rest.astype(BF16)
    low = (rest - mid.astype(F32)).astype(BF16)
    return high, mid, low


def lanes_of(x):
    return lax.broadcasted_iota(jnp.int32, x.shape, x.ndim - 1)


def edge_pair(first, last):
    return jnp.where(lanes_of(first) < 64, first, last)


def pack(pairs):
    packed = jnp.zeros_like(pairs[0])
    lane = lanes_of(packed)
    for n, pair in enumerate(pairs):
        packed = jnp.where(lane // 8 == n, pltpu.roll(pair, (8 * n + 4) % 128, 1), packed)
    return packed


def unpack(packed, n):
    return pltpu.roll(packed, (124 - 8 * n) % 128, 1)


def kernel(
    npx, nqy,
    rhs_hbm, x_hbm, dp_hbm, di_hbm, dr_hbm, bd_hbm, sg_hbm,
    basis, sol_out, res_out, weights_out,
    rhs_v, x_in, dp_v, di_v, dr_v, bd_v, sg_v,
    cx, ce, xx, p0, p1, p2, p3,
    x_out, x_side, f_out, f_side, h_out, h_side,
    rs_out, rs_buf, as_buf, ag_buf, packed_v,
    in_sem, c_send, c_recv, x_send, x_recv, h_send, h_recv, r_send, r_recv,
    sum_send, sum_recv,
):
    px, qy = lax.axis_index("px"), lax.axis_index("qy")
    y, x = px // CHIPS_X, px % CHIPS_X
    z, core = qy // CORES, qy % CORES
    ny, nz = npx // CHIPS_X, nqy // CORES
    nquad = nz // 2
    nnear, nfar = CHIPS_X * CORES * 2, ny * nquad
    near = (x * CORES + core) * 2 + z % 2
    far = y * nquad + z // 2

    def along_near(s):
        there = lax.rem(near + s, nnear)
        at_x, at_core, at_z = there // (2 * CORES), there // 2 % CORES, z - z % 2 + there % 2
        return there, {"px": y * CHIPS_X + at_x, "qy": at_z * CORES + at_core}

    def along_far(s):
        there = lax.rem(far + s, nfar)
        at_y, at_z = there // nquad, there % nquad * 2 + z % 2
        return there, {"px": at_y * CHIPS_X + x, "qy": at_z * CORES + core}

    def inside(a, b):
        return (px + a >= 0) & (px + a < npx) & (qy + b >= 0) & (qy + b < nqy)

    def device(a, b):
        return {"px": px + a, "qy": qy + b}

    barrier = pltpu.get_barrier_semaphore()
    count = jnp.int32(nnear + nfar - 2)
    for a, b in AROUND:
        count += inside(a, b).astype(jnp.int32)

        @pl.when(inside(a, b))
        def _():
            pl.semaphore_signal(barrier, inc=1, device_id=device(a, b), device_id_type=MESH)

    loads = []
    pairs = [(x_hbm.at[:, pl.ds(c * 128, 128)], x_in.at[c]) for c in range(TILES)]
    pairs += [(dp_hbm, dp_v), (di_hbm, di_v), (dr_hbm, dr_v), (bd_hbm, bd_v), (sg_hbm, sg_v)]
    pairs += [(rhs_hbm.at[:, pl.ds(c * 128, 128)], rhs_v.at[c]) for c in range(TILES)]
    for n, (src, dst) in enumerate(pairs):
        load = pltpu.make_async_copy(src, dst, in_sem.at[n])
        load.start()
        loads.append(load)

    for along, size in ((along_near, nnear), (along_far, nfar)):
        @pl.loop(1, size)
        def _(s):
            pl.semaphore_signal(barrier, inc=1, device_id=along(s)[1], device_id_type=MESH)

    for a, b in AROUND:
        @pl.when(jnp.logical_not(inside(a, b)))
        def _():
            if b == 0:
                edge = 0 if a < 0 else 24
                cx[:, pl.ds(edge, 8), :] = jnp.zeros((3, 8, COLS), F32)
                edge = 0 if a < 0 else ROWS + 1
                xx[edge, :, :, pl.ds(0, COLS)] = jnp.zeros((2, 8, COLS), F32)
                edge = 0 if a < 0 else HALO + ROWS
                for t in range(CYCLES):
                    p0[t, pl.ds(edge, HALO), :, :, pl.ds(0, COLS)] = (
                        jnp.zeros((HALO, 2, 8, COLS), F32)
                    )
                return
            s = 0 if b < 0 else 1
            tiles = {-1: (0,), 0: (1, 2), 1: (3,)}[a]
            for n in tiles:
                if a == 0:
                    x_side[s, n] = jnp.zeros((8, 128), F32)
                f_side[s, n] = jnp.zeros((8, 128), F32)
                for t in range(CYCLES):
                    h_side[t, s, n] = jnp.zeros((8, 128), F32)

    def start(copies):
        for (a, b), copy in copies:
            pl.when(inside(a, b))(copy.start)

    def arrive(copies):
        for (a, b), copy in copies:
            pl.when(inside(-a, -b))(copy.wait_recv)

    def leave(copies):
        for (a, b), copy in copies:
            pl.when(inside(a, b))(copy.wait_send)

    def remote(src, dst, send, recv, a, b):
        return (a, b), pltpu.make_async_remote_copy(
            src_ref=src, dst_ref=dst, send_sem=send, recv_sem=recv,
            device_id=device(a, b), device_id_type=MESH,
        )

    def edge_copies(out, side, send, recv, corners=True):
        beside, corner = [], []
        for n, (a, b) in enumerate(AROUND):
            if b == 0:
                continue
            s = 0 if b > 0 else 1
            if a == 0:
                beside.append(
                    remote(out, side.at[s, pl.ds(1, 2)], send.at[n], recv.at[n], a, b)
                )
            elif corners:
                from_tile, to_tile = (0, 3) if a < 0 else (1, 0)
                corner.append(
                    remote(out.at[from_tile], side.at[s, to_tile], send.at[n], recv.at[n], a, b)
                )
        return beside, corner

    def both_sides(side, tile):
        lane = lax.broadcasted_iota(jnp.int32, (8, 128), 1)
        return jnp.where(lane % 8 < 4, side[0, tile], side[1, tile])

    for load in loads[:TILES]:
        load.wait()

    def turn(i):
        for c in range(TILES):
            xx[1 + i, :, :, pl.ds(c * 128, 128)] = (
                x_in[c, pl.ds(i, NR, stride=ROWS), :].reshape(2, 8, 128)
            )

    for i in range(ROWS):
        turn(i)

    def pack_rows(ref, first, out):
        for tile in range(2):
            pairs = []
            for i in range(8):
                for h in range(2):
                    row = first + 8 * tile + i
                    pairs.append(
                        edge_pair(ref[row, h, :, pl.ds(0, 128)], ref[row, h, :, pl.ds(COLS - 128, 128)])
                    )
            out[tile] = pack(pairs)

    pack_rows(xx, 1, x_out)
    pl.semaphore_wait(barrier, count)
    x_rows = []
    for a in (-1, 1):
        n = AROUND.index((a, 0))
        x_rows.append(remote(
            xx.at[1 if a < 0 else ROWS, :, :, pl.ds(0, COLS)],
            xx.at[ROWS + 1 if a < 0 else 0, :, :, pl.ds(0, COLS)],
            x_send.at[n], x_recv.at[n], a, 0,
        ))
    x_beside, _ = edge_copies(x_out, x_side, x_send, x_recv, corners=False)
    start(x_beside)
    start(x_rows)

    for load in loads[TILES : TILES + 5]:
        load.wait()
    active = (1 - bd_v[...]).astype(F32)
    upward = sg_v[...].astype(F32)
    price = active * dp_v[...]
    lower = active * (di_v[...] + dr_v[...] * upward)
    higher = active * (di_v[...] + dr_v[...] * (1.0 - upward))
    own = pl.ds(8, ROWS)
    for n, field in enumerate((price, lower, higher)):
        cx[n, own, :] = field
    for tile in range(2):
        rows8 = slice(8 * tile, 8 * tile + 8)
        f_out[tile] = pack([
            edge_pair(field[rows8, :128], field[rows8, COLS - 128 :])
            for field in (price, lower, higher)
        ])
    f_rows = []
    for a in (-1, 1):
        n = AROUND.index((a, 0))
        f_rows.append(remote(
            cx.at[:, pl.ds(8 if a < 0 else 16, 8), :], cx.at[:, pl.ds(24 if a < 0 else 0, 8), :],
            c_send.at[n], c_recv.at[n], a, 0,
        ))
    f_beside, f_corner = edge_copies(f_out, f_side, c_send, c_recv)
    f_copies = f_beside + f_rows + f_corner
    start(f_copies)

    def spread(n, row, value, at, width):
        ce[n, row, :, pl.ds(at, width)] = jnp.broadcast_to(value, (8, width))

    diagonal = 1.0 + 2.0 * price + lower + higher
    for n, field in enumerate((diagonal, price, lower, higher)):
        for i in range(ROWS):
            spread(n, HALO + i, field[i : i + 1], 0, COLS)

    def image_row(above, center, below, row, width):
        def field(n):
            return ce[n, row, :, pl.ds(0, width)][None]

        def cut(value):
            return value[:, :, :width]

        return (
            field(0) * cut(center)
            - field(1) * (cut(above) + cut(below))
            - field(2) * cut(pltpu.roll(center, 1, 2))
            - field(3) * cut(pltpu.roll(center, WIDE - 1, 2))
        )

    for load in loads[TILES + 5 :]:
        load.wait()
    arrive(x_beside)
    for i in range(ROWS):
        tile = both_sides(x_side, 1 + i // 8)
        for h in range(2):
            xx[1 + i, h, :, pl.ds(COLS, 128)] = unpack(tile, 2 * (i % 8) + h)

    def first_residual(i):
        value = image_row(xx[i], xx[1 + i], xx[2 + i], HALO + i, COLS)
        for c in range(TILES):
            p0[0, HALO + i, :, :, pl.ds(c * 128, 128)] = (
                rhs_v[c, pl.ds(i, NR, stride=ROWS), :].reshape(2, 8, 128)
                - value[:, :, c * 128 : c * 128 + 128]
            )

    def rim_rows(t):
        copies = []
        for a in (-1, 1):
            for n in range(PIECES):
                begin = n * HALO // PIECES
                size = HALO // PIECES
                src = (HALO if a < 0 else ROWS) + begin
                dst = (HALO + ROWS if a < 0 else 0) + begin
                copies.append(remote(
                    p0.at[t, pl.ds(src, size), :, :, pl.ds(0, COLS)],
                    p0.at[t, pl.ds(dst, size), :, :, pl.ds(0, COLS)],
                    r_send.at[t, (a + 1) // 2, n], r_recv.at[t, (a + 1) // 2, n], a, 0,
                ))
        return copies

    def outer_rows_first(body, t, before_ends=None):
        for i in (1, 2, 3, 12, 13, 14):
            body(i)
        if before_ends is not None:
            before_ends()
        for i in (0, 15):
            body(i)
        if t < CYCLES:
            start(rim_rows(t))
        for i in range(HALO, ROWS - HALO):
            body(i)

    outer_rows_first(first_residual, 0, lambda: arrive(x_rows))

    def total(t, local):
        for j in range(nnear):
            rs_out[j] = local[2 * j : 2 * j + 2]
        rs_buf[t, near] = rs_out[near]

        def phase(n, along, size, src, buf, me):
            steps = [s for d in range(size // 2, 0, -1) for s in sorted({d, size - d})]
            for s in steps:
                there, where = along(s)
                pltpu.make_async_remote_copy(
                    src_ref=src(there), dst_ref=buf.at[t, me],
                    send_sem=sum_send.at[n], recv_sem=sum_recv.at[t, n],
                    device_id=where, device_id_type=MESH,
                ).start()
            whole = pltpu.make_async_remote_copy(
                src_ref=buf.at[t, pl.ds(0, size - 1)], dst_ref=buf.at[t, pl.ds(0, size - 1)],
                send_sem=sum_send.at[n], recv_sem=sum_recv.at[t, n],
                device_id={"px": px, "qy": qy}, device_id_type=MESH,
            )
            whole.wait_recv()
            return whole

        sent = [phase(0, along_near, nnear, lambda there: rs_out.at[there], rs_buf, near)]
        as_buf[t, far] = jnp.sum(rs_buf[t], axis=0)
        sent.append(phase(1, along_far, nfar, lambda there: as_buf.at[t, far], as_buf, far))
        ag_buf[t, near] = jnp.sum(as_buf[t], axis=0)
        sent.append(phase(2, along_near, nnear, lambda there: ag_buf.at[t, near], ag_buf, near))
        for j in range(nnear):
            packed_v[pl.ds(2 * j, 2), :] = ag_buf[t, j]
        return packed_v[...], sent

    def solve(both):
        tiles = [both[8 * r : 8 * r + 8] for r in range(8)]
        at = lax.broadcasted_iota(jnp.int32, (8, 128), 0)

        def across(row):
            return jnp.broadcast_to(row, (8, 128))

        for b in range(8):
            columns = [
                [jnp.broadcast_to(tile[:, n : n + 1], (8, 128)) for tile in tiles]
                for n in range(8 * b, 8 * b + 8)
            ]
            for j in range(8):
                pivots = columns[j]
                inverse = 1.0 / across(pivots[b][j : j + 1])

                def eliminate(group):
                    row = across(group[b][j : j + 1]) * inverse
                    after = [g - c * row for g, c in zip(group, pivots)]
                    after[b] = jnp.where(at == j, row, after[b])
                    return after

                for q in range(j + 1, 8):
                    columns[q] = eliminate(columns[q])
                tiles = eliminate(tiles)
        return jnp.concatenate(tiles, axis=0)

    def keep_limbs(i, block, value):
        for n, limb in enumerate(limbs(value[:, :, :COLS].reshape(NR, COLS))):
            basis[i, pl.ds(n * BASIS + block * NR, NR), :] = limb

    for t in range(CYCLES):
        last = t == CYCLES - 1
        fields = [p0.at[t], p1, p2, p3]
        rims = rim_rows(t)
        pack_rows(p0.at[t], HALO, h_out.at[t])
        beside, corner = edge_copies(h_out.at[t], h_side.at[t], h_send.at[t], h_recv.at[t])
        start(beside)
        start(corner)

        for i in range(ROWS):
            keep_limbs(i, STEPS, p0[t, HALO + i])

        if t == 0:
            arrive(f_copies)
            for p in range(EXT):
                row = 8 - HALO + p
                tile = both_sides(f_side, row // 8)
                values = [unpack(tile, n)[row % 8 : row % 8 + 1] for n in range(3)]
                values = [1.0 + 2.0 * values[0] + values[1] + values[2]] + values
                for n, value in enumerate(values):
                    spread(n, p, value, COLS, 128)
                if HALO <= p < HALO + ROWS:
                    continue
                values = [cx[n, pl.ds(row, 1), :] for n in range(3)]
                values = [1.0 + 2.0 * values[0] + values[1] + values[2]] + values
                for n, value in enumerate(values):
                    spread(n, p, value, 0, COLS)

        def lanes_around(p):
            row = 8 - HALO + p
            tile = both_sides(h_side.at[t], row // 8)
            for h in range(2):
                p0[t, p, h, :, pl.ds(COLS, 128)] = unpack(tile, 2 * (row % 8) + h)

        def advance(k, rows, inner):
            for p, own_row in zip(rows, inner):
                center = fields[k][p]
                image = image_row(
                    fields[k][p - 1], center, fields[k][p + 1], p,
                    WIDE if k < STEPS - 1 else COLS,
                )
                if k < STEPS - 1:
                    fields[k + 1][p] = image * (1.0 / THETA) - center * (SIGMA / THETA)
                if own_row:
                    keep_limbs(p - HALO, k, image)

        arrive(beside)
        for p in range(HALO, HALO + ROWS):
            lanes_around(p)
        for k in range(STEPS):
            rows = range(HALO + 1 + k, HALO + ROWS - 1 - k)
            advance(k, rows, [True] * len(rows))

        def gram_step(i, acc):
            for n in range(4):
                part = basis[4 * i + n]
                acc = acc + lax.dot_general(
                    part, part, (((1,), (1,)), ((), ())), preferred_element_type=F32
                )
            return acc

        acc = gram_step(2, gram_step(1, jnp.zeros((3 * BASIS, 3 * BASIS), F32)))

        arrive(rims)
        arrive(corner)
        for begin in (0, HALO + ROWS):
            for p in range(begin, begin + HALO):
                lanes_around(p)
        for k in range(STEPS):
            for begin in (k + 1, EXT - 5 - k):
                rows = [begin + n for n in range(4)]
                inner = [HALO <= p < HALO + ROWS for p in rows]
                advance(k, rows, inner)

        acc = gram_step(3, gram_step(0, acc))
        rows = acc[2 * BASIS :] + acc[BASIS : 2 * BASIS] + acc[:BASIS]
        gram = rows[:64, 2 * BASIS :] + rows[:64, BASIS : 2 * BASIS] + rows[:64, :BASIS]
        gram = jnp.concatenate([gram, jnp.zeros((64, 48), F32)], axis=1)
        lane = lax.broadcasted_iota(jnp.int32, (32, 128), 1)
        packed = jnp.where(lane < 80, gram[:32], pltpu.roll(gram[32:], 48, 1))
        packed, sent = total(t, packed)
        lower = pltpu.roll(packed, 80, 1)
        square = jnp.concatenate([packed, jnp.zeros((96, 128), F32)], axis=0)
        turned = square.T
        lower = jnp.where(lane < 32, turned[32:64], lower)
        answer = solve(jnp.concatenate([packed, lower], axis=0))
        if t == 0:
            leave(x_beside + x_rows + f_copies)
        leave(rims + beside + corner)
        for whole in sent:
            whole.wait_send()

        u = [answer[NR * k : NR * (k + 1)] for k in range(STEPS)]
        e = [None] * STEPS
        e[STEPS - 1] = u[STEPS - 1]
        for k in range(STEPS - 2, -1, -1):
            e[k] = u[k] - (SIGMA / THETA) * e[k + 1]
        lane = lax.broadcasted_iota(jnp.int32, (NR, 128), 1)
        blocks = []
        for k in range(STEPS + 1):
            to_res = -u[k] if k < STEPS else jnp.zeros_like(u[0])
            if k == STEPS:
                to_sol = e[0]
            elif k < STEPS - 1:
                to_sol = e[k + 1] * (1.0 / THETA)
            else:
                to_sol = jnp.zeros_like(u[0])
            blocks.append(jnp.where(lane < 80, to_res, pltpu.roll(to_sol, NR, 1)))
        blocks.append(jnp.zeros((48, 128), F32))
        weights = jnp.concatenate(blocks, axis=0).T[64:96, :BASIS]
        high, mid, low = limbs(weights)
        three = jnp.concatenate([high, mid, low], axis=0)
        three = jnp.concatenate([three] * 3, axis=1)

        if last:
            weights_out[...] = three
            break

        def update(i):
            change = combined(three, basis[i])
            res = p0[t, HALO + i, :, :, pl.ds(0, COLS)] + change[0]
            p0[t + 1, HALO + i, :, :, pl.ds(0, COLS)] = res
            res_out[i] = res
            sol_out[i] = xx[1 + i, :, :, pl.ds(0, COLS)] + change[1]

        outer_rows_first(update, t + 1)


def combined(weights, rows):
    parts = jnp.dot(weights, rows, preferred_element_type=F32)
    change = (parts[64:] + parts[32:64]) + parts[:32]
    width = rows.shape[-1]
    return change[:NR].reshape(2, 8, width), change[NR:].reshape(2, 8, width)


def finish(basis, sol_in, res_in, weights, sol_hbm, res_hbm, sol_v, res_v, sem):
    stores = []
    for begin in range(0, COLS, 256):
        cols = slice(begin, begin + 256)
        for i in range(ROWS):
            change = combined(weights[...], basis[i, :, cols])
            res, sol = res_in[i, :, :, cols] + change[0], sol_in[i, :, :, cols] + change[1]
            for c in range(2):
                part = slice(c * 128, c * 128 + 128)
                tile = begin // 128 + c
                res_v[tile, pl.ds(i, NR, stride=ROWS), :] = res[:, :, part].reshape(NR, 128)
                sol_v[tile, pl.ds(i, NR, stride=ROWS), :] = sol[:, :, part].reshape(NR, 128)
        for src, dst in ((sol_v, sol_hbm), (res_v, res_hbm)):
            for tile in (begin // 128, begin // 128 + 1):
                store = pltpu.make_async_copy(
                    src.at[tile], dst.at[:, pl.ds(tile * 128, 128)], sem.at[len(stores)]
                )
                store.start()
                stores.append(store)
    for store in stores:
        store.wait()


def solution(mesh):
    npx, nqy = mesh.shape["px"], mesh.shape["qy"]

    def per_device(rhs, iterate, *fields):
        flat = jax.ShapeDtypeStruct((NR * ROWS, COLS), F32)
        vmem = pltpu.VMEM
        dma = pltpu.SemaphoreType.DMA
        field = vmem((EXT, 2, 8, WIDE), F32)
        plane = vmem((ROWS, COLS), F32)
        marks = vmem((ROWS, COLS), jnp.int32)
        turned = vmem((TILES, NR * ROWS, 128), F32)
        sixteenth = vmem((CYCLES, 16, 2, 128), F32)
        held = jax.ShapeDtypeStruct((ROWS, 2, 8, COLS), F32)
        parts = pl.pallas_call(
            lambda *refs: kernel(npx, nqy, *refs),
            out_shape=(
                jax.ShapeDtypeStruct((ROWS, 3 * BASIS, COLS), BF16), held, held,
                jax.ShapeDtypeStruct((96, 3 * BASIS), BF16),
            ),
            in_specs=[pl.BlockSpec(memory_space=pl.ANY)] * 7,
            out_specs=(pl.BlockSpec(memory_space=vmem),) * 4,
            scratch_shapes=[
                turned, turned, plane, plane, plane, marks, marks,
                vmem((3, ROWS + 16, COLS), F32),
                vmem((4, EXT, 8, WIDE), F32),
                vmem((ROWS + 2, 2, 8, WIDE), F32),
                vmem((CYCLES, EXT, 2, 8, WIDE), F32),
                field, field, field,
                vmem((2, 8, 128), F32), vmem((2, 4, 8, 128), F32),
                vmem((2, 8, 128), F32), vmem((2, 4, 8, 128), F32),
                vmem((CYCLES, 2, 8, 128), F32), vmem((CYCLES, 2, 4, 8, 128), F32),
                vmem((16, 2, 128), F32), sixteenth, vmem((CYCLES, 32, 2, 128), F32), sixteenth,
                vmem((32, 128), F32),
                dma((5 + 2 * TILES,)),
                dma((8,)), dma((8,)), dma((8,)), dma((8,)),
                dma((CYCLES, 8)), dma((CYCLES, 8)),
                dma((CYCLES, 2, PIECES)), dma((CYCLES, 2, PIECES)),
                dma((3,)), dma((CYCLES, 3)),
            ],
            compiler_params=pltpu.CompilerParams(
                collective_id=0, has_side_effects=True, vmem_limit_bytes=48 * 1024 * 1024
            ),
        )(*[
            pltpu.with_memory_space_constraint(a, pltpu.HBM) for a in
            (rhs.reshape(NR * ROWS, COLS), iterate.reshape(NR * ROWS, COLS)) + fields
        ])
        sol, res = pl.pallas_call(
            finish,
            out_shape=(flat, flat),
            in_specs=[pl.BlockSpec(memory_space=vmem)] * 4,
            out_specs=(pl.BlockSpec(memory_space=pl.ANY),) * 2,
            scratch_shapes=[turned, turned, dma((2 * TILES,))],
            compiler_params=pltpu.CompilerParams(vmem_limit_bytes=48 * 1024 * 1024),
        )(*parts)
        return sol.reshape(NR, ROWS, COLS), res.reshape(NR, ROWS, COLS)

    whole, plane = P(None, "px", "qy"), P("px", "qy")
    return jax.shard_map(
        per_device, mesh=mesh, in_specs=(whole, whole) + (plane,) * 5,
        out_specs=(whole, whole), check_vma=False,
    )
```
